32 devices in a mesh: blk: 4 (over y, x), head: 4 (over z), grp: 2 (over core).
Axes of the slice: x: 2, y: 2, z: 4, core: 2. Of those that a mesh axis runs over, the one named last changes fastest.
Arguments:
- t_query: bfloat16 [4096, 4096], P('blk', ('head', 'grp')), may hold values from -80 to 80
- t_key: bfloat16 [4096, 4096], P('blk', ('head', 'grp')), may hold values from -80 to 80
- t_value: bfloat16 [4096, 4096], P('blk', ('head', 'grp')), may hold values from -6 to 6
- t_out: bfloat16 [4096, 4096], P(('head', 'grp')), may hold values from -0.09375 to 0.09375
- s_query: bfloat16 [4096, 2048], P('blk', ('head', 'grp')), may hold values from -80 to 80
- s_key: bfloat16 [4096, 2048], P('blk', ('head', 'grp')), may hold values from -80 to 80
- s_value: bfloat16 [4096, 2048], P('blk', ('head', 'grp')), may hold values from -6 to 6
- s_out: bfloat16 [2048, 4096], P(('head', 'grp')), may hold values from -0.125 to 0.125
- segments: int32 [4096], P('blk'), may hold values from 0 to 1, never falling along the last dimension, each value on 1 to 4032 neighbouring positions
- selection: int32 [64, 16], P('blk'), may hold values from 0 to 63, as said below
Outputs:
- mismatch: float32 [4096, 4096], P('blk', ('head', 'grp'))
- s_dq: float32 [4096, 2048], P('blk', ('head', 'grp'))
- s_dk: float32 [4096, 2048], P('blk', ('head', 'grp'))
- s_dv: float32 [4096, 2048], P('blk', ('head', 'grp'))
The draws below stay inside these ranges and needn't reach their ends.
Inputs may be any that keep to these rules, and one draw needn't show every extreme that they name: `selection`: entry 0 of row b is b itself; for b >= 32, entry 1 of row b is b - 32; every entry of row b lies between 0 and b; entries of a row may repeat. `segments`: document numbers never fall along the sequence.
All inputs are finite; a program needn't handle non-finite values.
Results may differ from the reference program's by a relative error of at most 0.015.
Values may be sent and summed in bfloat16 or wider, within the bound.
A program may use at most 128 MiB of HBM per device.

```python
import math
import jax
import jax.numpy as jnp
import numpy as np
from jax import lax

D = 4096
TH = 32
SH = 16
HD = 128
BS = 64
NSEL = 16
TOKENS = 4096
N_HEAD = 4
N_GRP = 2


def drawn_pair(key, columns, salt):
    folded = jax.random.fold_in(key, salt)
    key_rows = jax.random.normal(jax.random.fold_in(folded, 1), (TOKENS, columns), jnp.float32)
    queries = 2.5 * jax.random.normal(jax.random.fold_in(folded, 2), (TOKENS, columns), jnp.float32)
    return (queries.astype(jnp.bfloat16), key_rows.astype(jnp.bfloat16))


def draw_t_query(key, part):
    return drawn_pair(key, TH * HD, 101)[0]


def draw_t_key(key, part):
    return drawn_pair(key, TH * HD, 101)[1]


def draw_s_query(key, part):
    return drawn_pair(key, SH * HD, 202)[0]


def draw_s_key(key, part):
    return drawn_pair(key, SH * HD, 202)[1]


def draw_selection(key, part):
    block_count = TOKENS // BS
    rows = jnp.arange(block_count, dtype=jnp.int32)
    upper_bound = rows[:, None] + 1
    first_back = jax.random.randint(jax.random.fold_in(key, 303), (block_count, NSEL), 0, upper_bound, dtype=jnp.int32)
    second_back = jax.random.randint(jax.random.fold_in(key, 304), (block_count, NSEL), 0, upper_bound, dtype=jnp.int32)
    chosen = (rows[:, None] - jnp.minimum(first_back, second_back)).astype(jnp.int32)
    half = block_count // 2
    far_block = jnp.where(rows >= half, rows - half, chosen[:, 1]).astype(jnp.int32)
    chosen = chosen.at[:, 1].set(far_block)
    return chosen.at[:, 0].set(rows).astype(jnp.int32)


def shard_levels(stream_key, extent, split, low, high):
    loudness = 1.0
    for axis_at, parts in split:
        heights = jax.random.uniform(jax.random.fold_in(jax.random.fold_in(stream_key, 6), axis_at), (parts,), jnp.float32, low / len(split), high / len(split))
        loudness = loudness * jnp.repeat(jnp.exp(heights), extent[axis_at] // parts).reshape((-1,) + (1,) * (len(extent) - 1 - axis_at))
    return loudness


def length_profile(count, total, reach, skew):
    portions = [(1 << 20) // math.isqrt(grade ** skew) + 1 for grade in range(2, count + 1)]
    surplus, holding = total - reach - (count - 1), [1] * (count - 1)
    while surplus > 0:
        movable = [i for i in range(count - 1) if holding[i] < reach]
        pool, remaining = sum([portions[i] for i in movable]), surplus
        for i in movable:
            extra = min(reach - holding[i], max(1, remaining * portions[i] // pool), surplus)
            holding[i] = holding[i] + extra
            surplus = surplus - extra
    return np.array([reach] + holding)


def uneven_parts(own_key, number_of, total, reach, lean):
    if number_of == 2:
        one = jax.random.randint(own_key, (), max(1, total - reach), min(reach, total - 1) + 1)
        return jnp.stack([one, total - one])
    lengths = jnp.asarray(length_profile(number_of, total, reach, lean), jnp.int32)
    couples = (number_of - 1) // 2
    donor, taker = lengths[1:1 + 2 * couples:2], lengths[2:2 + 2 * couples:2]
    room = jnp.minimum(donor - 1, reach - taker)
    passed = jax.random.randint(jax.random.fold_in(own_key, 1), (couples,), 0, 1 << 20) % (room + 1)
    lengths = lengths.at[1:1 + 2 * couples:2].set(donor - passed).at[2:2 + 2 * couples:2].set(taker + passed)
    return lengths[jax.random.permutation(jax.random.fold_in(own_key, 2), number_of)]


def normal_values(own_key, shape, deviation, reach, cuts=(), kind=jnp.bfloat16):
    array = deviation * jax.random.normal(own_key, shape, jnp.float32)
    if cuts:
        array = array * shard_levels(own_key, shape, cuts, -0.22, 0.18)
    return jnp.clip(array, -reach, reach).astype(kind)


def setup_inputs(seed: int = 0) -> dict:
    splits = jax.random.split(jax.random.key(seed), 11)
    return {
        "t_query": draw_t_query(jax.random.fold_in(splits[10], 71), 0),
        "t_key": draw_t_key(jax.random.fold_in(splits[10], 71), 0),
        "t_value": normal_values(splits[2], (TOKENS, TH * HD), 1.0, 6.0, ((0, 4), (1, 8))),
        "t_out": normal_values(splits[3], (TH * HD, D), (TH * HD) ** -0.5, 0.09375, ((0, 8),)),
        "s_query": draw_s_query(jax.random.fold_in(splits[10], 71), 0),
        "s_key": draw_s_key(jax.random.fold_in(splits[10], 71), 0),
        "s_value": normal_values(splits[6], (TOKENS, SH * HD), 1.0, 6.0, ((0, 4), (1, 8))),
        "s_out": normal_values(splits[7], (SH * HD, D), (SH * HD) ** -0.5, 0.125, ((0, 8),)),
        "segments": jnp.searchsorted(jnp.cumsum(uneven_parts(splits[8], 2, TOKENS, TOKENS - BS, 0)), jnp.arange(TOKENS), side="right").astype(jnp.int32),
        "selection": draw_selection(jax.random.fold_in(splits[10], 71), 0),
    }


masked_score = -1e+30

def teacher_head(queries, key_rows, value_rows, segment_all):
    positions = jnp.arange(queries.shape[0]).astype(jnp.int32)
    scores = jnp.dot(queries, key_rows.T, preferred_element_type=jnp.float32) * HD ** (-0.5)
    allowed = (positions[None, :] <= positions[:, None]) & (segment_all[None, :] == segment_all[:, None])
    scores = jnp.where(allowed, scores, masked_score)
    largest = lax.optimization_barrier(jnp.max(scores, axis=1, keepdims=True))
    weights = jnp.where(allowed, jnp.exp(scores - largest), 0.0)
    running = lax.optimization_barrier(jnp.sum(weights, axis=1, keepdims=True))
    blended = jnp.dot(weights.astype(jnp.bfloat16), value_rows, preferred_element_type=jnp.float32)
    return (blended / running).astype(jnp.bfloat16)

def student_attn(queries, key_all, value_all, segment_all, selection, first_row):
    row_count = queries.shape[0]
    head_count = queries.shape[1] // HD
    blocks = row_count // BS
    query_blocks = queries.reshape(blocks, BS, head_count, HD)
    key_blocks = key_all.reshape(-1, BS, head_count, HD)[selection].reshape(blocks, NSEL * BS, head_count, HD)
    value_blocks = value_all.reshape(-1, BS, head_count, HD)[selection].reshape(blocks, NSEL * BS, head_count, HD)
    key_pos = (selection[:, :, None] * BS + jnp.arange(BS).astype(jnp.int32)[None, None, :]).astype(jnp.int32).reshape(blocks, NSEL * BS)
    query_pos = (first_row + jnp.arange(row_count).astype(jnp.int32)).astype(jnp.int32).reshape(blocks, BS)
    key_seg = segment_all[key_pos]
    query_seg = segment_all[query_pos]
    scores = jnp.einsum('bqhd,bkhd->bhqk', query_blocks, key_blocks, precision=lax.Precision.HIGHEST) * HD ** (-0.5)
    allowed = ((key_pos[:, None, :] <= query_pos[:, :, None]) & (key_seg[:, None, :] == query_seg[:, :, None]))[:, None]
    scores = jnp.where(allowed, scores, masked_score)
    largest = lax.stop_gradient(lax.optimization_barrier(jnp.max(scores, axis=3, keepdims=True)))
    weights = jnp.where(allowed, jnp.exp(scores - largest), 0.0)
    weights = weights / lax.optimization_barrier(jnp.sum(weights, axis=3, keepdims=True))
    blended = jnp.einsum('bhqk,bkhd->bqhd', weights, value_blocks, precision=lax.Precision.HIGHEST)
    return blended.reshape(row_count, head_count * HD)

def reference(t_query, t_key, t_value, t_out, s_query, s_key, s_value, s_out, segments, selection):
    tokens = t_query.shape[0]

    def heads_first(matrix):
        return matrix.reshape(tokens, -1, HD).transpose(1, 0, 2)

    def heads_last(matrix):
        return matrix.transpose(1, 0, 2).reshape(tokens, -1)
    teacher = lax.map(lambda triple: teacher_head(triple[0], triple[1], triple[2], segments), (heads_first(t_query), heads_first(t_key), heads_first(t_value)))
    t_attn = heads_last(teacher)
    student_inputs = (heads_first(s_query.astype(jnp.float32)), heads_first(s_key.astype(jnp.float32)), heads_first(s_value.astype(jnp.float32)))

    def student_forward(triple):
        return student_attn(triple[0], triple[1], triple[2], segments, selection, 0)
    s_attn = heads_last(lax.map(student_forward, student_inputs)).astype(jnp.bfloat16)
    groups = N_HEAD * N_GRP
    teacher_cols = TH * HD // groups
    student_cols = SH * HD // groups
    mismatch = jnp.zeros((tokens, D), jnp.float32)
    for group_index in range(groups):
        student_part = jnp.dot(s_attn[:, group_index * student_cols:(group_index + 1) * student_cols], s_out[group_index * student_cols:(group_index + 1) * student_cols], preferred_element_type=jnp.float32)
        teacher_part = jnp.dot(t_attn[:, group_index * teacher_cols:(group_index + 1) * teacher_cols], t_out[group_index * teacher_cols:(group_index + 1) * teacher_cols], preferred_element_type=jnp.float32)
        rounded = lax.optimization_barrier((student_part - teacher_part).astype(jnp.bfloat16))
        mismatch = mismatch + rounded.astype(jnp.float32)
    grad_out = jnp.dot(mismatch.astype(jnp.bfloat16), s_out.T, preferred_element_type=jnp.float32)

    def student_backward(quadruple):

        def local_attn(first, second, third):
            return student_attn(first, second, third, segments, selection, 0)
        _, pullback = jax.vjp(local_attn, quadruple[0], quadruple[1], quadruple[2])
        return pullback(quadruple[3])
    grad_query, grad_keys, grad_values = lax.map(student_backward, student_inputs + (heads_first(grad_out),))
    return (mismatch, heads_last(grad_query), heads_last(grad_keys), heads_last(grad_values))
```

```python
import functools

import jax
import jax.numpy as jnp
from jax import lax
from jax.experimental import pallas as pl
from jax.experimental.pallas import tpu as pltpu
from jax.sharding import PartitionSpec as P

HD = 128
BS = 64
SCALE = HD ** (-0.5)
LOG2E = 1.4426950408889634
MASKED = -1e30
VMEM_LIMIT = 56 * 1024 * 1024

NT = (((1,), (1,)), ((), ()))
TN = (((0,), (0,)), ((), ()))


def dot(a, b, dims=(((1,), (0,)), ((), ()))):
    return lax.dot_general(a, b, dims, preferred_element_type=jnp.float32)


def visible(key_pos, query_pos, first_count):
    low = jnp.where(query_pos < first_count, 0, first_count)
    return (key_pos <= query_pos) & (key_pos >= low)


def teacher_kernel(tile, info_ref, q_ref, k_ref, v_ref, o_ref):
    offset, first_count = info_ref[0], info_ref[1]
    q_tile = q_ref.shape[0]
    q_start = offset + pl.program_id(1) * q_tile
    q_end = q_start + q_tile
    queries = q_ref[...]

    def step(index, carried, masked):
        largest, total, acc = carried
        rows = pl.ds(pl.multiple_of(index * tile, tile), tile)
        scores = dot(k_ref[rows, :], queries, NT)
        if masked:
            key_pos = index * tile + lax.broadcasted_iota(jnp.int32, scores.shape, 0)
            query_pos = q_start + lax.broadcasted_iota(jnp.int32, (1, q_tile), 1)
            scores = jnp.where(visible(key_pos, query_pos, first_count), scores, MASKED)
        new = jnp.maximum(largest, jnp.max(scores, axis=0, keepdims=True))
        weights = jnp.exp2((scores - new) * (SCALE * LOG2E))
        if masked:
            weights = jnp.where(scores > 0.5 * MASKED, weights, 0.0)
        factor = jnp.exp2((largest - new) * (SCALE * LOG2E))
        total = total * factor + jnp.sum(weights, axis=0, keepdims=True)
        acc = acc * factor + dot(v_ref[rows, :], weights.astype(jnp.bfloat16), TN)
        return new, total, acc

    first = jnp.where(q_start >= first_count, first_count // tile, 0)
    last = (q_end + tile - 1) // tile
    straddles = first_count < q_end

    def general(index, carried):
        low, high = index * tile, (index + 1) * tile
        need = (high > q_start) | ((low < first_count) & straddles)
        return lax.cond(
            need,
            lambda c: step(index, c, True),
            lambda c: step(index, c, False),
            carried,
        )

    carried = (
        jnp.full((1, q_tile), MASKED, jnp.float32),
        jnp.zeros((1, q_tile), jnp.float32),
        jnp.zeros((HD, q_tile), jnp.float32),
    )
    _, total, acc = lax.fori_loop(first, last, general, carried)
    o_ref[...] = (acc / total).T.astype(jnp.bfloat16)


def teacher(queries, keys, values, heads, columns, offset, first_count):
    rows, tokens = queries.shape[0], keys.shape[0]
    width = heads * HD
    step, (q_at, k_at, v_at) = columns
    tile = 512
    info = jnp.stack([offset, first_count]).astype(jnp.int32)
    return pl.pallas_call(
        functools.partial(teacher_kernel, tile),
        grid_spec=pltpu.PrefetchScalarGridSpec(
            num_scalar_prefetch=1,
            grid=(heads, rows // tile),
            in_specs=[
                pl.BlockSpec((tile, HD), lambda h, i, s: (i, step * h + q_at)),
                pl.BlockSpec((tokens, HD), lambda h, i, s: (0, step * h + k_at)),
                pl.BlockSpec((tokens, HD), lambda h, i, s: (0, step * h + v_at)),
            ],
            out_specs=pl.BlockSpec((tile, HD), lambda h, i, s: (i, h)),
        ),
        out_shape=jax.ShapeDtypeStruct((rows, width), jnp.bfloat16),
        compiler_params=pltpu.CompilerParams(vmem_limit_bytes=VMEM_LIMIT),
        cost_estimate=pl.CostEstimate(
            flops=2 * rows * tokens * width, bytes_accessed=8 * tokens * width, transcendentals=0
        ),
    )(info, queries, keys, values)


def spread(ref, scratch, heads):
    for h in range(heads):
        cols = slice(h * HD, (h + 1) * HD)
        scratch[h * BS : (h + 1) * BS, cols] = ref[:, cols].astype(scratch.dtype)


def student_weights(sel_ref, place_ref, info_ref, q_wide, k_all, v_all, k_sel, v_sel, pos, heads):
    block = pl.program_id(0)
    count = sel_ref.shape[1]
    offset, first_count = info_ref[0], info_ref[1]
    within = lax.broadcasted_iota(jnp.int32, (BS, 1), 0)
    for e in range(count):
        chosen = sel_ref[block, e]
        source = pl.ds(pl.multiple_of(place_ref[block, e] * BS, BS), BS)
        k_sel[e * BS : (e + 1) * BS, :] = k_all[source, :]
        v_sel[e * BS : (e + 1) * BS, :] = v_all[source, :]
        pos[e * BS : (e + 1) * BS, :] = jnp.broadcast_to(chosen * BS + within, (BS, heads * BS))
    lane = lax.broadcasted_iota(jnp.int32, (1, heads * BS), 1)
    query_pos = offset + block * BS + lax.rem(lane, BS)
    scores = dot(k_sel[...], q_wide[...], NT)
    allowed = visible(pos[...], query_pos, first_count)
    scores = jnp.where(allowed, scores, MASKED)
    largest = jnp.max(scores, axis=0, keepdims=True)
    weights = jnp.exp2((scores - largest) * (SCALE * LOG2E))
    weights = jnp.where(allowed, weights, 0.0)
    return weights, jnp.sum(weights, axis=0, keepdims=True)


def forward_kernel(heads, sel_ref, place_ref, info_ref, q_ref, k_all, v_all, o_ref, q_wide, k_sel, v_sel, pos):
    @pl.when(pl.program_id(0) == 0)
    def _():
        q_wide[...] = jnp.zeros_like(q_wide)

    spread(q_ref, q_wide, heads)
    weights, total = student_weights(
        sel_ref, place_ref, info_ref, q_wide, k_all, v_all, k_sel, v_sel, pos, heads
    )
    weights = (weights / total).astype(jnp.bfloat16)
    blended = dot(weights, v_sel[...], TN)
    for h in range(heads):
        cols = slice(h * HD, (h + 1) * HD)
        o_ref[:, cols] = blended[h * BS : (h + 1) * BS, cols].astype(jnp.bfloat16)


def backward_kernel(
    heads, cycle, sel_ref, place_ref, info_ref, q_ref, g_ref, k_all, v_all, dq_ref, *rest
):
    own_ref, far_refs = rest[0], rest[1:cycle]
    dk_sum, dv_sum, q_wide, g_wide, k_sel, v_sel, pos = rest[cycle:]
    block = pl.program_id(0)

    @pl.when(block == 0)
    def _():
        q_wide[...] = jnp.zeros_like(q_wide)
        g_wide[...] = jnp.zeros_like(g_wide)
        dk_sum[...] = jnp.zeros_like(dk_sum)
        dv_sum[...] = jnp.zeros_like(dv_sum)

    spread(q_ref, q_wide, heads)
    spread(g_ref, g_wide, heads)
    weights, total = student_weights(
        sel_ref, place_ref, info_ref, q_wide, k_all, v_all, k_sel, v_sel, pos, heads
    )
    weights = weights / total
    weight_grad = dot(v_sel[...], g_wide[...], NT)
    row_dots = jnp.sum(weights * weight_grad, axis=0, keepdims=True)
    score_grad = (weights * (weight_grad - row_dots) * SCALE).astype(jnp.bfloat16)
    query_grad = dot(score_grad, k_sel[...], TN)
    for h in range(heads):
        cols = slice(h * HD, (h + 1) * HD)
        dq_ref[:, cols] = query_grad[h * BS : (h + 1) * BS, cols]
    key_grad = dot(score_grad, q_wide[...])
    value_grad = dot(weights.astype(jnp.bfloat16), g_wide[...])
    for e in range(sel_ref.shape[1]):
        target = pl.ds(pl.multiple_of(place_ref[block, e] * BS, BS), BS)
        dk_sum[target, :] += key_grad[e * BS : (e + 1) * BS, :]
        dv_sum[target, :] += value_grad[e * BS : (e + 1) * BS, :]

    @pl.when(block == pl.num_programs(0) - 1)
    def _():
        rows = own_ref.shape[1]
        own_ref[0] = dk_sum[:rows, :]
        own_ref[1] = dv_sum[:rows, :]
        for d in range(1, cycle):
            far_refs[d - 1][0] = dk_sum[d * rows : (d + 1) * rows, :].astype(jnp.bfloat16)
            far_refs[d - 1][1] = dv_sum[d * rows : (d + 1) * rows, :].astype(jnp.bfloat16)


def student_scratch(heads, keys, wides):
    width = heads * HD
    return [pltpu.VMEM((heads * BS, width), jnp.bfloat16)] * wides + [
        pltpu.VMEM((keys, width), jnp.bfloat16),
        pltpu.VMEM((keys, width), jnp.bfloat16),
        pltpu.VMEM((keys, heads * BS), jnp.int32),
    ]


def student_forward(tables, queries, keys, values):
    rows, width = queries.shape
    tokens = keys.shape[0]
    heads = width // HD
    row_block = pl.BlockSpec((BS, width), lambda b, *_: (b, 0))
    whole = pl.BlockSpec((tokens, width), lambda b, *_: (0, 0))
    return pl.pallas_call(
        functools.partial(forward_kernel, heads),
        grid_spec=pltpu.PrefetchScalarGridSpec(
            num_scalar_prefetch=3,
            grid=(rows // BS,),
            in_specs=[row_block, whole, whole],
            out_specs=row_block,
            scratch_shapes=student_scratch(heads, tables[0].shape[1] * BS, 1),
        ),
        out_shape=jax.ShapeDtypeStruct((rows, width), jnp.bfloat16),
        compiler_params=pltpu.CompilerParams(vmem_limit_bytes=VMEM_LIMIT),
        cost_estimate=pl.CostEstimate(
            flops=16 * rows * tokens * width, bytes_accessed=4 * tokens * width, transcendentals=0
        ),
    )(*tables, queries, keys, values)


def student_backward(tables, queries, grads, keys, values):
    rows, width = queries.shape
    tokens = keys.shape[0]
    cycle = tokens // rows
    heads = width // HD
    row_block = pl.BlockSpec((BS, width), lambda b, *_: (b, 0))
    whole = pl.BlockSpec((tokens, width), lambda b, *_: (0, 0))
    pair = pl.BlockSpec((2, rows, width), lambda b, *_: (0, 0, 0))
    return pl.pallas_call(
        functools.partial(backward_kernel, heads, cycle),
        grid_spec=pltpu.PrefetchScalarGridSpec(
            num_scalar_prefetch=3,
            grid=(rows // BS,),
            in_specs=[row_block, row_block, whole, whole],
            out_specs=[row_block] + [pair] * cycle,
            scratch_shapes=[pltpu.VMEM((tokens, width), jnp.float32)] * 2
            + student_scratch(heads, tables[0].shape[1] * BS, 2),
        ),
        out_shape=[
            jax.ShapeDtypeStruct((rows, width), jnp.float32),
            jax.ShapeDtypeStruct((2, rows, width), jnp.float32),
        ]
        + [jax.ShapeDtypeStruct((2, rows, width), jnp.bfloat16)] * (cycle - 1),
        compiler_params=pltpu.CompilerParams(vmem_limit_bytes=VMEM_LIMIT),
        cost_estimate=pl.CostEstimate(
            flops=32 * rows * tokens * width, bytes_accessed=8 * tokens * width, transcendentals=0
        ),
    )(*tables, queries, grads, keys, values)


def project_kernel(s_attn, t_attn, s_out, t_out, o_ref):
    o_ref[0] = (dot(s_attn[...], s_out[...]) - dot(t_attn[...], t_out[...])).astype(jnp.bfloat16)


def project(s_attn, t_attn, s_out, t_out, groups):
    rows = s_attn.shape[0]
    model = s_out.shape[1]
    tile = model // groups
    return pl.pallas_call(
        project_kernel,
        grid=(groups,),
        in_specs=[
            pl.BlockSpec(s_attn.shape, lambda j: (0, 0)),
            pl.BlockSpec(t_attn.shape, lambda j: (0, 0)),
            pl.BlockSpec((s_attn.shape[1], tile), lambda j: (0, j)),
            pl.BlockSpec((t_attn.shape[1], tile), lambda j: (0, j)),
        ],
        out_specs=pl.BlockSpec((1, rows, tile), lambda j: (j, 0, 0)),
        out_shape=jax.ShapeDtypeStruct((groups, rows, tile), jnp.bfloat16),
        compiler_params=pltpu.CompilerParams(vmem_limit_bytes=VMEM_LIMIT),
    )(s_attn, t_attn, s_out, t_out)


def project_grads_kernel(t_width, s_attn, t_attn, mix, o_ref):
    pieces, rows, width = mix.shape
    columns = mix[...].reshape(pieces * rows, width)
    o_ref[0] = (
        dot(s_attn[...], columns[:, t_width:], NT) - dot(t_attn[...], columns[:, :t_width], NT)
    ).astype(jnp.bfloat16)


def project_grads(s_attn, t_attn, mix, groups):
    rows = s_attn.shape[0]
    pieces, depth, width = mix.shape
    tile = depth // groups
    return pl.pallas_call(
        functools.partial(project_grads_kernel, t_attn.shape[1]),
        grid=(groups,),
        in_specs=[
            pl.BlockSpec(s_attn.shape, lambda j: (0, 0)),
            pl.BlockSpec(t_attn.shape, lambda j: (0, 0)),
            pl.BlockSpec((pieces, tile, width), lambda j: (0, j, 0)),
        ],
        out_specs=pl.BlockSpec((1, rows, pieces * tile), lambda j: (j, 0, 0)),
        out_shape=jax.ShapeDtypeStruct((groups, rows, pieces * tile), jnp.bfloat16),
        compiler_params=pltpu.CompilerParams(vmem_limit_bytes=VMEM_LIMIT),
    )(s_attn, t_attn, mix)


def from_earlier(rows, distance):
    route = [(i - distance, i) for i in range(distance, lax.axis_size("blk"))]
    return lax.ppermute(rows, "blk", route)


def on_device(t_query, t_key, t_value, t_out, s_query, s_key, s_value, s_out, segments, selection):
    row_count = t_query.shape[0]
    heads = t_query.shape[1] // HD
    cycle = lax.axis_size("blk")
    split = ("head", "grp")
    groups = lax.axis_size("head") * lax.axis_size("grp")
    my_index = lax.axis_index("blk")
    first_row = my_index * row_count
    shard_blocks = row_count // BS

    count = jnp.sum((segments == 0).astype(jnp.int32)).reshape(1)
    first_count = count
    for distance in range(1, cycle):
        route = [(i, (i + distance) % cycle) for i in range(cycle)]
        first_count = first_count + lax.ppermute(count, "blk", route)
    first_count = first_count[0]
    info = jnp.stack([first_row, first_count]).astype(jnp.int32)

    piece = s_out.shape[0] // cycle
    s_rows = lax.dynamic_slice_in_dim(s_out, my_index * piece, piece, 0)
    s_rows = lax.all_gather(s_rows, split, axis=0, tiled=True)
    mix = jnp.concatenate([dot(s_rows, t_out, NT), dot(s_rows, s_out, NT)], axis=1)
    mix = lax.all_gather(mix.astype(jnp.bfloat16), "blk")

    if heads % cycle == 0:
        packed = jnp.concatenate(
            [rows.reshape(row_count, heads, HD) for rows in (t_query, t_key, t_value)], axis=2
        ).reshape(row_count, 3 * heads * HD)
        packed = lax.all_to_all(packed, "blk", split_axis=1, concat_axis=0, tiled=True)
        packed, s_key, s_value = lax.optimization_barrier((packed, s_key, s_value))
        whole_heads = teacher(
            packed, packed, packed, heads // cycle, (3, (0, 1, 2)), jnp.int32(0), first_count
        )
        t_attn = lax.all_to_all(whole_heads, "blk", split_axis=0, concat_axis=1, tiled=True)
    else:
        t_attn = teacher(
            t_query,
            lax.all_gather(t_key, "blk", axis=0, tiled=True),
            lax.all_gather(t_value, "blk", axis=0, tiled=True),
            heads,
            (1, (0, 0, 0)),
            first_row,
            first_count,
        )

    key_stack = jnp.concatenate([s_key] + [from_earlier(s_key, d) for d in range(1, cycle)])
    value_stack = jnp.concatenate([s_value] + [from_earlier(s_value, d) for d in range(1, cycle)])
    place = (my_index - selection // shard_blocks) * shard_blocks + selection % shard_blocks
    tables = (selection, place, info)
    s_attn = student_forward(tables, s_query, key_stack, value_stack)

    grad_terms = project_grads(s_attn, t_attn, mix, groups)
    grads = lax.psum_scatter(grad_terms, split, scatter_dimension=0, tiled=False)
    terms = project(s_attn, t_attn, s_out, t_out, groups)
    terms, grads = lax.optimization_barrier((terms, grads))
    mismatch = lax.psum_scatter(terms, split, scatter_dimension=0, tiled=False)

    grad_query, own, *far = student_backward(
        tables, s_query, grads, key_stack, value_stack
    )
    for distance in range(1, cycle):
        route = [(i, i - distance) for i in range(distance, cycle)]
        own = own + lax.ppermute(far[distance - 1], "blk", route).astype(jnp.float32)
    return (mismatch.astype(jnp.float32), grad_query, own[0], own[1])


def solution(mesh):
    split = ("head", "grp")
    tokens, weights = P("blk", split), P(split, None)
    return jax.shard_map(
        on_device,
        mesh=mesh,
        in_specs=(
            tokens, tokens, tokens, weights, tokens, tokens, tokens, weights, P("blk"),
            P("blk", None),
        ),
        out_specs=(tokens,) * 4,
        check_vma=False,
    )
```

```python
import functools

import jax
import jax.numpy as jnp
from jax import lax
from jax.experimental import pallas as pl
from jax.experimental.pallas import tpu as pltpu
from jax.sharding import PartitionSpec as P

HD = 128
BS = 64
SCALE = HD ** (-0.5)
LOG2E = 1.4426950408889634
MASKED = -1e30
VMEM_LIMIT = 56 * 1024 * 1024

NT = (((1,), (1,)), ((), ()))
TN = (((0,), (0,)), ((), ()))


def dot(a, b, dims=(((1,), (0,)), ((), ()))):
    return lax.dot_general(a, b, dims, preferred_element_type=jnp.float32)


def visible(key_pos, query_pos, first_count):
    low = jnp.where(query_pos < first_count, 0, first_count)
    return (key_pos <= query_pos) & (key_pos >= low)


def teacher_kernel(tile, info_ref, q_ref, k_ref, v_ref, o_ref):
    offset, first_count = info_ref[0], info_ref[1]
    q_tile = q_ref.shape[0]
    q_start = offset + pl.program_id(1) * q_tile
    q_end = q_start + q_tile
    queries = q_ref[...]

    def step(index, carried, masked):
        largest, total, acc = carried
        rows = pl.ds(pl.multiple_of(index * tile, tile), tile)
        scores = dot(k_ref[rows, :], queries, NT)
        if masked:
            key_pos = index * tile + lax.broadcasted_iota(jnp.int32, scores.shape, 0)
            query_pos = q_start + lax.broadcasted_iota(jnp.int32, (1, q_tile), 1)
            scores = jnp.where(visible(key_pos, query_pos, first_count), scores, MASKED)
        new = jnp.maximum(largest, jnp.max(scores, axis=0, keepdims=True))
        weights = jnp.exp2((scores - new) * (SCALE * LOG2E))
        if masked:
            weights = jnp.where(scores > 0.5 * MASKED, weights, 0.0)
        factor = jnp.exp2((largest - new) * (SCALE * LOG2E))
        total = total * factor + jnp.sum(weights, axis=0, keepdims=True)
        acc = acc * factor + dot(v_ref[rows, :], weights.astype(jnp.bfloat16), TN)
        return new, total, acc

    first = jnp.where(q_start >= first_count, first_count // tile, 0)
    last = (q_end + tile - 1) // tile
    straddles = first_count < q_end

    def general(index, carried):
        low, high = index * tile, (index + 1) * tile
        need = (high > q_start) | ((low < first_count) & straddles)
        return lax.cond(
            need,
            lambda c: step(index, c, True),
            lambda c: step(index, c, False),
            carried,
        )

    carried = (
        jnp.full((1, q_tile), MASKED, jnp.float32),
        jnp.zeros((1, q_tile), jnp.float32),
        jnp.zeros((HD, q_tile), jnp.float32),
    )
    _, total, acc = lax.fori_loop(first, last, general, carried)
    o_ref[...] = (acc / total).T.astype(jnp.bfloat16)


def teacher(queries, keys, values, heads, columns, offset, first_count):
    rows, tokens = queries.shape[0], keys.shape[0]
    width = heads * HD
    step, (q_at, k_at, v_at) = columns
    tile = 512
    info = jnp.stack([offset, first_count]).astype(jnp.int32)
    return pl.pallas_call(
        functools.partial(teacher_kernel, tile),
        grid_spec=pltpu.PrefetchScalarGridSpec(
            num_scalar_prefetch=1,
            grid=(heads, rows // tile),
            in_specs=[
                pl.BlockSpec((tile, HD), lambda h, i, s: (i, step * h + q_at)),
                pl.BlockSpec((tokens, HD), lambda h, i, s: (0, step * h + k_at)),
                pl.BlockSpec((tokens, HD), lambda h, i, s: (0, step * h + v_at)),
            ],
            out_specs=pl.BlockSpec((tile, HD), lambda h, i, s: (i, h)),
        ),
        out_shape=jax.ShapeDtypeStruct((rows, width), jnp.bfloat16),
        compiler_params=pltpu.CompilerParams(vmem_limit_bytes=VMEM_LIMIT),
        cost_estimate=pl.CostEstimate(
            flops=2 * rows * tokens * width, bytes_accessed=8 * tokens * width, transcendentals=0
        ),
    )(info, queries, keys, values)


def spread(ref, scratch, heads):
    for h in range(heads):
        cols = slice(h * HD, (h + 1) * HD)
        scratch[h * BS : (h + 1) * BS, cols] = ref[:, cols].astype(scratch.dtype)


def student_weights(sel_ref, place_ref, info_ref, q_wide, k_all, v_all, k_sel, v_sel, pos, heads):
    block = pl.program_id(0)
    count = sel_ref.shape[1]
    offset, first_count = info_ref[0], info_ref[1]
    within = lax.broadcasted_iota(jnp.int32, (BS, 1), 0)
    for e in range(count):
        chosen = sel_ref[block, e]
        source = pl.ds(pl.multiple_of(place_ref[block, e] * BS, BS), BS)
        k_sel[e * BS : (e + 1) * BS, :] = k_all[source, :]
        v_sel[e * BS : (e + 1) * BS, :] = v_all[source, :]
        pos[e * BS : (e + 1) * BS, :] = jnp.broadcast_to(chosen * BS + within, (BS, heads * BS))
    lane = lax.broadcasted_iota(jnp.int32, (1, heads * BS), 1)
    query_pos = offset + block * BS + lax.rem(lane, BS)
    scores = dot(k_sel[...], q_wide[...], NT)
    allowed = visible(pos[...], query_pos, first_count)
    scores = jnp.where(allowed, scores, MASKED)
    largest = jnp.max(scores, axis=0, keepdims=True)
    weights = jnp.exp2((scores - largest) * (SCALE * LOG2E))
    weights = jnp.where(allowed, weights, 0.0)
    return weights, jnp.sum(weights, axis=0, keepdims=True)


def forward_kernel(heads, sel_ref, place_ref, info_ref, q_ref, k_all, v_all, o_ref, q_wide, k_sel, v_sel, pos):
    @pl.when(pl.program_id(0) == 0)
    def _():
        q_wide[...] = jnp.zeros_like(q_wide)

    spread(q_ref, q_wide, heads)
    weights, total = student_weights(
        sel_ref, place_ref, info_ref, q_wide, k_all, v_all, k_sel, v_sel, pos, heads
    )
    weights = (weights / total).astype(jnp.bfloat16)
    blended = dot(weights, v_sel[...], TN)
    for h in range(heads):
        cols = slice(h * HD, (h + 1) * HD)
        o_ref[:, cols] = blended[h * BS : (h + 1) * BS, cols].astype(jnp.bfloat16)


def backward_kernel(
    heads, cycle, sel_ref, place_ref, info_ref, q_ref, g_ref, k_all, v_all, dq_ref, *rest
):
    own_ref, far_refs = rest[0], rest[1:cycle]
    dk_sum, dv_sum, q_wide, g_wide, k_sel, v_sel, pos = rest[cycle:]
    block = pl.program_id(0)

    @pl.when(block == 0)
    def _():
        q_wide[...] = jnp.zeros_like(q_wide)
        g_wide[...] = jnp.zeros_like(g_wide)
        dk_sum[...] = jnp.zeros_like(dk_sum)
        dv_sum[...] = jnp.zeros_like(dv_sum)

    spread(q_ref, q_wide, heads)
    spread(g_ref, g_wide, heads)
    weights, total = student_weights(
        sel_ref, place_ref, info_ref, q_wide, k_all, v_all, k_sel, v_sel, pos, heads
    )
    weights = weights / total
    weight_grad = dot(v_sel[...], g_wide[...], NT)
    row_dots = jnp.sum(weights * weight_grad, axis=0, keepdims=True)
    score_grad = (weights * (weight_grad - row_dots) * SCALE).astype(jnp.bfloat16)
    query_grad = dot(score_grad, k_sel[...], TN)
    for h in range(heads):
        cols = slice(h * HD, (h + 1) * HD)
        dq_ref[:, cols] = query_grad[h * BS : (h + 1) * BS, cols]
    key_grad = dot(score_grad, q_wide[...])
    value_grad = dot(weights.astype(jnp.bfloat16), g_wide[...])
    for e in range(sel_ref.shape[1]):
        target = pl.ds(pl.multiple_of(place_ref[block, e] * BS, BS), BS)
        dk_sum[target, :] += key_grad[e * BS : (e + 1) * BS, :]
        dv_sum[target, :] += value_grad[e * BS : (e + 1) * BS, :]

    @pl.when(block == pl.num_programs(0) - 1)
    def _():
        rows = own_ref.shape[1]
        own_ref[0] = dk_sum[:rows, :]
        own_ref[1] = dv_sum[:rows, :]
        for d in range(1, cycle):
            far_refs[d - 1][0] = dk_sum[d * rows : (d + 1) * rows, :].astype(jnp.bfloat16)
            far_refs[d - 1][1] = dv_sum[d * rows : (d + 1) * rows, :].astype(jnp.bfloat16)


def student_scratch(heads, keys, wides):
    width = heads * HD
    return [pltpu.VMEM((heads * BS, width), jnp.bfloat16)] * wides + [
        pltpu.VMEM((keys, width), jnp.bfloat16),
        pltpu.VMEM((keys, width), jnp.bfloat16),
        pltpu.VMEM((keys, heads * BS), jnp.int32),
    ]


def student_forward(tables, queries, keys, values):
    rows, width = queries.shape
    tokens = keys.shape[0]
    heads = width // HD
    row_block = pl.BlockSpec((BS, width), lambda b, *_: (b, 0))
    whole = pl.BlockSpec((tokens, width), lambda b, *_: (0, 0))
    return pl.pallas_call(
        functools.partial(forward_kernel, heads),
        grid_spec=pltpu.PrefetchScalarGridSpec(
            num_scalar_prefetch=3,
            grid=(rows // BS,),
            in_specs=[row_block, whole, whole],
            out_specs=row_block,
            scratch_shapes=student_scratch(heads, tables[0].shape[1] * BS, 1),
        ),
        out_shape=jax.ShapeDtypeStruct((rows, width), jnp.bfloat16),
        compiler_params=pltpu.CompilerParams(vmem_limit_bytes=VMEM_LIMIT),
        cost_estimate=pl.CostEstimate(
            flops=16 * rows * tokens * width, bytes_accessed=4 * tokens * width, transcendentals=0
        ),
    )(*tables, queries, keys, values)


def student_backward(tables, queries, grads, keys, values):
    rows, width = queries.shape
    tokens = keys.shape[0]
    cycle = tokens // rows
    heads = width // HD
    row_block = pl.BlockSpec((BS, width), lambda b, *_: (b, 0))
    whole = pl.BlockSpec((tokens, width), lambda b, *_: (0, 0))
    pair = pl.BlockSpec((2, rows, width), lambda b, *_: (0, 0, 0))
    return pl.pallas_call(
        functools.partial(backward_kernel, heads, cycle),
        grid_spec=pltpu.PrefetchScalarGridSpec(
            num_scalar_prefetch=3,
            grid=(rows // BS,),
            in_specs=[row_block, row_block, whole, whole],
            out_specs=[row_block] + [pair] * cycle,
            scratch_shapes=[pltpu.VMEM((tokens, width), jnp.float32)] * 2
            + student_scratch(heads, tables[0].shape[1] * BS, 2),
        ),
        out_shape=[
            jax.ShapeDtypeStruct((rows, width), jnp.float32),
            jax.ShapeDtypeStruct((2, rows, width), jnp.float32),
        ]
        + [jax.ShapeDtypeStruct((2, rows, width), jnp.bfloat16)] * (cycle - 1),
        compiler_params=pltpu.CompilerParams(vmem_limit_bytes=VMEM_LIMIT),
        cost_estimate=pl.CostEstimate(
            flops=32 * rows * tokens * width, bytes_accessed=8 * tokens * width, transcendentals=0
        ),
    )(*tables, queries, grads, keys, values)


def project_kernel(s_attn, t_attn, s_out, t_out, o_ref):
    o_ref[0] = (dot(s_attn[...], s_out[...]) - dot(t_attn[...], t_out[...])).astype(jnp.bfloat16)


def project(s_attn, t_attn, s_out, t_out, groups):
    rows = s_attn.shape[0]
    model = s_out.shape[1]
    tile = model // groups
    return pl.pallas_call(
        project_kernel,
        grid=(groups,),
        in_specs=[
            pl.BlockSpec(s_attn.shape, lambda j: (0, 0)),
            pl.BlockSpec(t_attn.shape, lambda j: (0, 0)),
            pl.BlockSpec((s_attn.shape[1], tile), lambda j: (0, j)),
            pl.BlockSpec((t_attn.shape[1], tile), lambda j: (0, j)),
        ],
        out_specs=pl.BlockSpec((1, rows, tile), lambda j: (j, 0, 0)),
        out_shape=jax.ShapeDtypeStruct((groups, rows, tile), jnp.bfloat16),
        compiler_params=pltpu.CompilerParams(vmem_limit_bytes=VMEM_LIMIT),
    )(s_attn, t_attn, s_out, t_out)


def project_grads_kernel(t_width, s_attn, t_attn, mix, o_ref):
    pieces, rows, width = mix.shape
    columns = mix[...].reshape(pieces * rows, width)
    o_ref[0] = (
        dot(s_attn[...], columns[:, t_width:], NT) - dot(t_attn[...], columns[:, :t_width], NT)
    ).astype(jnp.bfloat16)


def project_grads(s_attn, t_attn, mix, groups):
    rows = s_attn.shape[0]
    pieces, depth, width = mix.shape
    tile = depth // groups
    return pl.pallas_call(
        functools.partial(project_grads_kernel, t_attn.shape[1]),
        grid=(groups,),
        in_specs=[
            pl.BlockSpec(s_attn.shape, lambda j: (0, 0)),
            pl.BlockSpec(t_attn.shape, lambda j: (0, 0)),
            pl.BlockSpec((pieces, tile, width), lambda j: (0, j, 0)),
        ],
        out_specs=pl.BlockSpec((1, rows, pieces * tile), lambda j: (j, 0, 0)),
        out_shape=jax.ShapeDtypeStruct((groups, rows, pieces * tile), jnp.bfloat16),
        compiler_params=pltpu.CompilerParams(vmem_limit_bytes=VMEM_LIMIT),
    )(s_attn, t_attn, mix)


def from_earlier(rows, distance):
    route = [(i - distance, i) for i in range(distance, lax.axis_size("blk"))]
    return lax.ppermute(rows, "blk", route)


MESH = pl.DeviceIdType.MESH


def greet(blk, grp, cycle, cores):
    barrier = pltpu.get_barrier_semaphore()
    for d in range(cycle):
        for e in range(cores):
            if d or e:
                pl.semaphore_signal(
                    barrier,
                    inc=1,
                    device_id={"blk": lax.rem(blk + d, cycle), "grp": lax.rem(grp + e, cores)},
                    device_id_type=MESH,
                )
    pl.semaphore_wait(barrier, cycle * cores - 1)


def send(src, dst, send_sem, recv_sem, blk, grp):
    return pltpu.make_async_remote_copy(
        src_ref=src,
        dst_ref=dst,
        send_sem=send_sem,
        recv_sem=recv_sem,
        device_id={"blk": blk, "grp": grp},
        device_id_type=MESH,
    )


def arrive_kernel(
    cycle, cores, tq, tk, tv, sq, sk, sv, ints,
    oq, ok, ov, pq, pk, pv, oints,
    t_stage, s_stage, local, s_send, s_recv, x_send, x_recv, t_send, t_recv, i_send, i_recv,
):
    blk, grp = lax.axis_index("blk"), lax.axis_index("grp")
    rows = tq.shape[0]
    half = rows // cores
    share = cycle // cores
    owner = blk // share
    greet(blk, grp, cycle, cores)

    def student_copy(t, j, e):
        src = (sq, sk, sv)[t].at[pl.ds(e * half, half), pl.ds(j * HD, HD)]
        dst = (pq.at[blk], pk.at[e, blk], pv.at[e, blk])[t]
        return src, dst

    def student_send(t, j, e):
        return send(
            *student_copy(t, j, e), s_send.at[t, j, e], s_recv.at[t, blk], grp * share + j, e
        )

    pieces = [(t, j, e) for t in (1, 2, 0) for j in range(share) for e in range(cores)]
    for t, j, e in pieces:
        mine = (grp * share + j == blk) & (grp == e)

        @pl.when(jnp.logical_not(mine))
        def _():
            student_send(t, j, e).start()

    int_copies = [
        send(ints, oints.at[blk], i_send.at[d - 1], i_recv.at[d - 1], lax.rem(blk + d, cycle), grp)
        for d in range(1, cycle)
    ]
    for copy in int_copies:
        copy.start()
    oints[blk] = ints[...]

    t_copies = []
    for t, (src, dst) in enumerate(((tk, ok), (tv, ov), (tq, oq))):
        for d in range(1, cycle):
            dest = lax.rem(blk + d, cycle)
            columns = pl.ds(pl.multiple_of(dest * HD, HD), HD)
            t_copies.append(
                send(
                    src.at[:, columns], dst.at[blk], t_send.at[t, d - 1], t_recv.at[t, d - 1], dest, grp
                )
            )
    for copy in t_copies:
        copy.start()

    columns = pl.ds(pl.multiple_of(blk * HD, HD), HD)
    for t, (src, dst) in enumerate(((tk, ok), (tv, ov), (tq, oq))):
        pltpu.make_async_copy(src.at[:, columns], t_stage.at[t], local.at[t]).start()
    for t, (src, dst) in enumerate(((tk, ok), (tv, ov), (tq, oq))):
        pltpu.make_async_copy(src.at[:, columns], t_stage.at[t], local.at[t]).wait()
        pltpu.make_async_copy(t_stage.at[t], dst.at[blk], local.at[t]).start()
    for t, (src, dst) in enumerate(((tk, ok), (tv, ov), (tq, oq))):
        pltpu.make_async_copy(t_stage.at[t], dst.at[blk], local.at[t]).wait()

    for t, j, e in pieces:
        mine = (grp * share + j == blk) & (grp == e)

        @pl.when(mine)
        def _():
            src, dst = student_copy(t, j, e)
            inward = pltpu.make_async_copy(src, s_stage, local.at[0])
            inward.start()
            inward.wait()
            outward = pltpu.make_async_copy(s_stage, dst, local.at[0])
            outward.start()
            outward.wait()

    other = lax.rem(grp + 1, cores)

    def arrival(t, s):
        dst = (pq.at[s], pk.at[grp, s], pv.at[grp, s])[t]
        return send(dst, dst, s_send.at[t, 0, 0], s_recv.at[t, s], other, other)

    def cross(t, s):
        ref = (None, pk, pv)[t].at[grp, s]
        return send(ref, ref, x_send.at[t - 1, s], x_recv.at[t - 1, s], blk, other)

    for t in (1, 2, 0):
        for s in range(cycle):
            remote = jnp.logical_not((s == blk) & (owner == grp))

            @pl.when(remote)
            def _():
                arrival(t, s).wait_recv()

            if t:
                cross(t, s).start()

    for t in (1, 2):
        for s in range(cycle):
            cross(t, s).wait()
    for copy in int_copies + t_copies:
        copy.wait()
    for t, j, e in pieces:
        mine = (grp * share + j == blk) & (grp == e)

        @pl.when(jnp.logical_not(mine))
        def _():
            student_send(t, j, e).wait_send()


def arrive(t_query, t_key, t_value, s_query, s_key, s_value, ints, cycle, cores):
    rows = t_query.shape[0]
    half = rows // cores
    share = cycle // cores
    kind = t_query.dtype
    any_space = pl.BlockSpec(memory_space=pl.ANY)
    vmem = pl.BlockSpec(memory_space=pltpu.VMEM)
    dma = pltpu.SemaphoreType.DMA
    return pl.pallas_call(
        functools.partial(arrive_kernel, cycle, cores),
        in_specs=[any_space] * 6 + [vmem],
        out_specs=[any_space] * 6 + [vmem],
        out_shape=[jax.ShapeDtypeStruct((cycle, rows, HD), kind)] * 3
        + [jax.ShapeDtypeStruct((cycle, half, HD), kind)]
        + [jax.ShapeDtypeStruct((cores, cycle, half, HD), kind)] * 2
        + [jax.ShapeDtypeStruct((cycle,) + ints.shape, ints.dtype)],
        scratch_shapes=[
            pltpu.VMEM((3, rows, HD), kind),
            pltpu.VMEM((half, HD), kind),
            dma((3,)),
            dma((3, share, cores)),
            dma((3, cycle)),
            dma((2, cycle)),
            dma((2, cycle)),
            dma((3, cycle - 1)),
            dma((3, cycle - 1)),
            dma((cycle - 1,)),
            dma((cycle - 1,)),
        ],
        compiler_params=pltpu.CompilerParams(
            collective_id=0, has_side_effects=True, vmem_limit_bytes=VMEM_LIMIT
        ),
        cost_estimate=pl.CostEstimate(
            flops=0, bytes_accessed=64 * rows * HD * 2 * cycle, transcendentals=0
        ),
    )(t_query, t_key, t_value, s_query, s_key, s_value, ints)


def depart_kernel(cycle, cores, dq, own, far, out, got, mine, x_send, x_recv, d_send, d_recv):
    blk, grp = lax.axis_index("blk"), lax.axis_index("grp")
    half = dq.shape[1]
    share = cycle // cores
    owner, slot = blk // share, lax.rem(blk, share)
    other = lax.rem(grp + 1, cores)
    greet(blk, grp, cycle, cores)

    def target(t, j, e):
        rows = pl.ds(pl.multiple_of(e * half, half), half)
        return out.at[t, rows, pl.ds(pl.multiple_of(j * HD, HD), HD)]

    def source(t, s):
        return dq.at[s] if t == 0 else mine.at[t - 1, s]

    def piece(t, s):
        return send(
            source(t, s), target(t, slot, grp), d_send.at[t, s], d_recv.at[t, slot, grp], s, owner
        )

    def local(s):
        return (s == blk) & (owner == grp)

    def emit(t, s):
        @pl.when(jnp.logical_not(local(s)))
        def _():
            piece(t, s).start()

        @pl.when(local(s))
        def _():
            target(t, slot, grp)[...] = source(t, s)[...]

    crossing = [
        send(far.at[t], got.at[t], x_send.at[t], x_recv.at[t], blk, other) for t in range(2)
    ]
    for copy in crossing:
        copy.start()
    for s in range(cycle):
        emit(0, s)
    for t in range(2):
        crossing[t].wait_recv()
        for s in range(cycle):
            mine[t, s] = (own[t, s] + got[t, s].astype(jnp.float32)).astype(jnp.bfloat16)
        for s in range(cycle):
            emit(t + 1, s)
    for copy in crossing:
        copy.wait_send()
    for t in range(3):
        for j in range(share):
            for e in range(cores):
                ours = (grp * share + j == blk) & (grp == e)

                @pl.when(jnp.logical_not(ours))
                def _():
                    ref = target(t, j, e)
                    send(ref, ref, d_send.at[t, 0], d_recv.at[t, j, e], blk, other).wait_recv()

    for t in range(3):
        for s in range(cycle):
            @pl.when(jnp.logical_not(local(s)))
            def _():
                piece(t, s).wait_send()


def depart(dq, own, far, cycle, cores):
    half = dq.shape[1]
    share = cycle // cores
    vmem = pl.BlockSpec(memory_space=pltpu.VMEM)
    dma = pltpu.SemaphoreType.DMA
    return pl.pallas_call(
        functools.partial(depart_kernel, cycle, cores),
        in_specs=[vmem] * 3,
        out_specs=vmem,
        out_shape=jax.ShapeDtypeStruct((3, cores * half, share * HD), jnp.bfloat16),
        scratch_shapes=[
            pltpu.VMEM((2, cycle, half, HD), jnp.bfloat16),
            pltpu.VMEM((2, cycle, half, HD), jnp.bfloat16),
            dma((2,)),
            dma((2,)),
            dma((3, cycle)),
            dma((3, share, cores)),
        ],
        compiler_params=pltpu.CompilerParams(
            collective_id=1, has_side_effects=True, vmem_limit_bytes=VMEM_LIMIT
        ),
    )(dq, own, far)


def pair_weights(sel_ref, place_ref, info_ref, per_blk, q_wide, k_all, v_all, k_sel, v_sel):
    pair = pl.program_id(0)
    count = sel_ref.shape[1]
    first_count, grp = info_ref[0], info_ref[1]
    mine = per_blk // info_ref[2]

    def query_block(index):
        return (index // mine) * per_blk + grp * mine + lax.rem(index, mine)

    for e in range(count):
        for h in range(2):
            source = pl.ds(pl.multiple_of(place_ref[2 * pair + h, e] * BS, BS), BS)
            cols = slice(h * HD, (h + 1) * HD)
            k_sel[e * BS : (e + 1) * BS, cols] = k_all[source, :]
            v_sel[e * BS : (e + 1) * BS, cols] = v_all[source, :]
    within = lax.broadcasted_iota(jnp.int32, (BS, 1), 0)
    lane = lax.broadcasted_iota(jnp.int32, (1, 2 * BS), 1)
    second = lane >= BS
    query_pos = (
        jnp.where(second, query_block(2 * pair + 1), query_block(2 * pair)) * BS + lax.rem(lane, BS)
    )
    low = jnp.where(query_pos < first_count, 0, first_count)
    scores = dot(k_sel[...], q_wide[...], NT)
    allowed = []
    for e in range(count):
        base = jnp.where(second, sel_ref[2 * pair + 1, e], sel_ref[2 * pair, e]) * BS
        allowed.append((within <= query_pos - base) & (within >= low - base))
    scores = jnp.concatenate(
        [jnp.where(a, scores[e * BS : (e + 1) * BS], MASKED) for e, a in enumerate(allowed)]
    )
    largest = jnp.max(scores, axis=0, keepdims=True)
    weights = jnp.exp2((scores - largest) * (SCALE * LOG2E))
    weights = jnp.concatenate(
        [jnp.where(a, weights[e * BS : (e + 1) * BS], 0.0) for e, a in enumerate(allowed)]
    )
    return weights, jnp.sum(weights, axis=0, keepdims=True)


def spread_pair(ref, scratch):
    for h in range(2):
        scratch[h * BS : (h + 1) * BS, h * HD : (h + 1) * HD] = ref[h * BS : (h + 1) * BS, :].astype(
            scratch.dtype
        )


def pair_forward_kernel(
    per_blk, sel_ref, place_ref, info_ref, q_ref, k_all, v_all, o_ref, q_wide, k_sel, v_sel
):
    @pl.when(pl.program_id(0) == 0)
    def _():
        q_wide[...] = jnp.zeros_like(q_wide)

    spread_pair(q_ref, q_wide)
    weights, total = pair_weights(
        sel_ref, place_ref, info_ref, per_blk, q_wide, k_all, v_all, k_sel, v_sel
    )
    weights = (weights / total).astype(jnp.bfloat16)
    blended = dot(weights, v_sel[...], TN)
    for h in range(2):
        o_ref[h * BS : (h + 1) * BS, :] = blended[
            h * BS : (h + 1) * BS, h * HD : (h + 1) * HD
        ].astype(jnp.bfloat16)


def pair_backward_kernel(
    per_blk, sel_ref, place_ref, info_ref, q_ref, g_ref, k_all, v_all, dq_ref, own_ref, far_ref,
    dk_sum, dv_sum, q_wide, g_wide, k_sel, v_sel,
):
    pair = pl.program_id(0)

    @pl.when(pair == 0)
    def _():
        q_wide[...] = jnp.zeros_like(q_wide)
        g_wide[...] = jnp.zeros_like(g_wide)
        dk_sum[...] = jnp.zeros_like(dk_sum)
        dv_sum[...] = jnp.zeros_like(dv_sum)

    spread_pair(q_ref, q_wide)
    spread_pair(g_ref, g_wide)
    weights, total = pair_weights(
        sel_ref, place_ref, info_ref, per_blk, q_wide, k_all, v_all, k_sel, v_sel
    )
    weights = weights / total
    weight_grad = dot(v_sel[...], g_wide[...], NT)
    row_dots = jnp.sum(weights * weight_grad, axis=0, keepdims=True)
    score_grad = (weights * (weight_grad - row_dots) * SCALE).astype(jnp.bfloat16)
    query_grad = dot(score_grad, k_sel[...], TN)
    for h in range(2):
        dq_ref[h * BS : (h + 1) * BS, :] = query_grad[
            h * BS : (h + 1) * BS, h * HD : (h + 1) * HD
        ].astype(jnp.bfloat16)
    key_grad = dot(score_grad, q_wide[...])
    value_grad = dot(weights.astype(jnp.bfloat16), g_wide[...])
    for e in range(sel_ref.shape[1]):
        for h in range(2):
            target = pl.ds(pl.multiple_of(place_ref[2 * pair + h, e] * BS, BS), BS)
            cols = slice(h * HD, (h + 1) * HD)
            dk_sum[target, :] += key_grad[e * BS : (e + 1) * BS, cols]
            dv_sum[target, :] += value_grad[e * BS : (e + 1) * BS, cols]

    @pl.when(pair == pl.num_programs(0) - 1)
    def _():
        part = own_ref.shape[1]
        near = pl.ds(pl.multiple_of(info_ref[1] * part, part), part)
        away = pl.ds(pl.multiple_of((info_ref[2] - 1 - info_ref[1]) * part, part), part)
        own_ref[0] = dk_sum[near, :]
        own_ref[1] = dv_sum[near, :]
        far_ref[0] = dk_sum[away, :].astype(jnp.bfloat16)
        far_ref[1] = dv_sum[away, :].astype(jnp.bfloat16)


def pair_scratch(keys, wides):
    return [pltpu.VMEM((2 * BS, 2 * HD), jnp.bfloat16)] * wides + [
        pltpu.VMEM((keys, 2 * HD), jnp.bfloat16),
        pltpu.VMEM((keys, 2 * HD), jnp.bfloat16),
    ]


def pair_forward(per_blk, tables, queries, keys, values):
    rows, width = queries.shape
    tokens = keys.shape[0]
    row_block = pl.BlockSpec((2 * BS, width), lambda b, *_: (b, 0))
    whole = pl.BlockSpec((tokens, width), lambda b, *_: (0, 0))
    return pl.pallas_call(
        functools.partial(pair_forward_kernel, per_blk),
        grid_spec=pltpu.PrefetchScalarGridSpec(
            num_scalar_prefetch=3,
            grid=(rows // (2 * BS),),
            in_specs=[row_block, whole, whole],
            out_specs=row_block,
            scratch_shapes=pair_scratch(tables[0].shape[1] * BS, 1),
        ),
        out_shape=jax.ShapeDtypeStruct((rows, width), jnp.bfloat16),
        compiler_params=pltpu.CompilerParams(vmem_limit_bytes=VMEM_LIMIT),
        cost_estimate=pl.CostEstimate(
            flops=16 * rows * tokens * width, bytes_accessed=4 * tokens * width, transcendentals=0
        ),
    )(*tables, queries, keys, values)


def pair_backward(per_blk, cores, tables, queries, grads, keys, values):
    rows, width = queries.shape
    tokens = keys.shape[0]
    part = tokens // cores
    row_block = pl.BlockSpec((2 * BS, width), lambda b, *_: (b, 0))
    whole = pl.BlockSpec((tokens, width), lambda b, *_: (0, 0))
    both = pl.BlockSpec((2, part, width), lambda b, *_: (0, 0, 0))
    return pl.pallas_call(
        functools.partial(pair_backward_kernel, per_blk),
        grid_spec=pltpu.PrefetchScalarGridSpec(
            num_scalar_prefetch=3,
            grid=(rows // (2 * BS),),
            in_specs=[row_block, row_block, whole, whole],
            out_specs=[row_block, both, both],
            scratch_shapes=[pltpu.VMEM((tokens, width), jnp.float32)] * 2
            + pair_scratch(tables[0].shape[1] * BS, 2),
        ),
        out_shape=[
            jax.ShapeDtypeStruct((rows, width), jnp.bfloat16),
            jax.ShapeDtypeStruct((2, part, width), jnp.float32),
            jax.ShapeDtypeStruct((2, part, width), jnp.bfloat16),
        ],
        compiler_params=pltpu.CompilerParams(vmem_limit_bytes=VMEM_LIMIT),
        cost_estimate=pl.CostEstimate(
            flops=32 * rows * tokens * width, bytes_accessed=8 * tokens * width, transcendentals=0
        ),
    )(*tables, queries, grads, keys, values)


def heads_on_chips(
    t_query, t_key, t_value, t_out, s_query, s_key, s_value, s_out, segments, selection
):
    rows = t_query.shape[0]
    cycle, cores = lax.axis_size("blk"), lax.axis_size("grp")
    split = ("head", "grp")
    groups = lax.axis_size("head") * cores
    blk, grp = lax.axis_index("blk"), lax.axis_index("grp")
    half = rows // cores
    share = cycle // cores
    per_blk = rows // BS
    mine = per_blk // cores
    picks = selection.shape[1]

    piece = s_out.shape[0] // cycle
    s_rows = lax.dynamic_slice_in_dim(s_out, blk * piece, piece, 0)
    s_rows = lax.all_gather(s_rows, split, axis=0, tiled=True)

    lanes = 128
    ints = jnp.concatenate(
        [segments.reshape(rows // lanes, lanes), jnp.pad(selection, ((0, 0), (0, lanes - picks)))]
    )
    tq, tk, tv, pq, pk, pv, ints = arrive(
        t_query, t_key, t_value, s_query, s_key, s_value, ints, cycle, cores
    )
    s_rows, tq = lax.optimization_barrier((s_rows, tq))
    seg_rows = rows // lanes
    first_count = jnp.sum((ints[:, :seg_rows] == 0).astype(jnp.int32))
    info = jnp.stack([first_count, grp, jnp.int32(cores)]).astype(jnp.int32)
    chosen = lax.dynamic_slice_in_dim(ints[:, seg_rows:, :picks], grp * mine, mine, 1)
    chosen = chosen.reshape(cycle * mine, picks)
    at = chosen % per_blk
    place = ((at // mine) * cycle + chosen // per_blk) * mine + at % mine
    tables = (chosen, place, info)
    pq = pq.reshape(cycle * half, HD)
    pk, pv = pk.reshape(cycle * rows, HD), pv.reshape(cycle * rows, HD)

    blended = pair_forward(per_blk, tables, pq, pk, pv)
    tables, blended, tq = lax.optimization_barrier((tables, blended, tq))
    blended = lax.all_to_all(blended.reshape(cycle, half, HD), "blk", 0, 0, tiled=True)
    blended = lax.all_to_all(blended, "grp", split_axis=0, concat_axis=1, tiled=True)
    s_attn = blended.transpose(1, 0, 2).reshape(rows, share * HD)

    mix = jnp.concatenate([dot(s_rows, t_out, NT), dot(s_rows, s_out, NT)], axis=1)
    mix = lax.all_gather(mix.astype(jnp.bfloat16), "blk")

    whole = [x.reshape(cycle * rows, HD) for x in (tq, tk, tv)]
    whole_heads = teacher(*whole, 1, (1, (0, 0, 0)), jnp.int32(0), first_count)
    t_attn = lax.all_to_all(whole_heads, "blk", split_axis=0, concat_axis=1, tiled=True)

    grad_terms = project_grads(s_attn, t_attn, mix, groups)
    grads = lax.psum_scatter(grad_terms, split, scatter_dimension=0, tiled=False)
    terms = project(s_attn, t_attn, s_out, t_out, groups)
    terms, grads = lax.optimization_barrier((terms, grads))
    mismatch = lax.psum_scatter(terms, split, scatter_dimension=0, tiled=False)

    grads = grads.reshape(rows, share, HD).transpose(1, 0, 2)
    grads = lax.all_to_all(grads, "grp", split_axis=1, concat_axis=0, tiled=True)
    grads = lax.all_to_all(grads, "blk", 0, 0, tiled=True).reshape(cycle * half, HD)
    dq, own, far = pair_backward(per_blk, cores, tables, pq, grads, pk, pv)
    out = depart(
        dq.reshape(cycle, half, HD),
        own.reshape(2, cycle, half, HD),
        far.reshape(2, cycle, half, HD),
        cycle,
        cores,
    ).astype(jnp.float32)
    return (mismatch.astype(jnp.float32), out[0], out[1], out[2])


def on_device(t_query, t_key, t_value, t_out, s_query, s_key, s_value, s_out, segments, selection):
    row_count = t_query.shape[0]
    heads = t_query.shape[1] // HD
    cycle = lax.axis_size("blk")
    split = ("head", "grp")
    groups = lax.axis_size("head") * lax.axis_size("grp")
    cores = lax.axis_size("grp")
    if cores == 2 and heads == cycle and s_query.shape[1] // HD * cores == cycle:
        return heads_on_chips(
            t_query, t_key, t_value, t_out, s_query, s_key, s_value, s_out, segments, selection
        )
    my_index = lax.axis_index("blk")
    first_row = my_index * row_count
    shard_blocks = row_count // BS

    count = jnp.sum((segments == 0).astype(jnp.int32)).reshape(1)
    first_count = count
    for distance in range(1, cycle):
        route = [(i, (i + distance) % cycle) for i in range(cycle)]
        first_count = first_count + lax.ppermute(count, "blk", route)
    first_count = first_count[0]
    info = jnp.stack([first_row, first_count]).astype(jnp.int32)

    piece = s_out.shape[0] // cycle
    s_rows = lax.dynamic_slice_in_dim(s_out, my_index * piece, piece, 0)
    s_rows = lax.all_gather(s_rows, split, axis=0, tiled=True)
    mix = jnp.concatenate([dot(s_rows, t_out, NT), dot(s_rows, s_out, NT)], axis=1)
    mix = lax.all_gather(mix.astype(jnp.bfloat16), "blk")

    if heads % cycle == 0:
        packed = jnp.concatenate(
            [rows.reshape(row_count, heads, HD) for rows in (t_query, t_key, t_value)], axis=2
        ).reshape(row_count, 3 * heads * HD)
        packed = lax.all_to_all(packed, "blk", split_axis=1, concat_axis=0, tiled=True)
        packed, s_key, s_value = lax.optimization_barrier((packed, s_key, s_value))
        whole_heads = teacher(
            packed, packed, packed, heads // cycle, (3, (0, 1, 2)), jnp.int32(0), first_count
        )
        t_attn = lax.all_to_all(whole_heads, "blk", split_axis=0, concat_axis=1, tiled=True)
    else:
        t_attn = teacher(
            t_query,
            lax.all_gather(t_key, "blk", axis=0, tiled=True),
            lax.all_gather(t_value, "blk", axis=0, tiled=True),
            heads,
            (1, (0, 0, 0)),
            first_row,
            first_count,
        )

    key_stack = jnp.concatenate([s_key] + [from_earlier(s_key, d) for d in range(1, cycle)])
    value_stack = jnp.concatenate([s_value] + [from_earlier(s_value, d) for d in range(1, cycle)])
    place = (my_index - selection // shard_blocks) * shard_blocks + selection % shard_blocks
    tables = (selection, place, info)
    s_attn = student_forward(tables, s_query, key_stack, value_stack)

    grad_terms = project_grads(s_attn, t_attn, mix, groups)
    grads = lax.psum_scatter(grad_terms, split, scatter_dimension=0, tiled=False)
    terms = project(s_attn, t_attn, s_out, t_out, groups)
    terms, grads = lax.optimization_barrier((terms, grads))
    mismatch = lax.psum_scatter(terms, split, scatter_dimension=0, tiled=False)

    grad_query, own, *far = student_backward(
        tables, s_query, grads, key_stack, value_stack
    )
    for distance in range(1, cycle):
        route = [(i, i - distance) for i in range(distance, cycle)]
        own = own + lax.ppermute(far[distance - 1], "blk", route).astype(jnp.float32)
    return (mismatch.astype(jnp.float32), grad_query, own[0], own[1])


def solution(mesh):
    split = ("head", "grp")
    tokens, weights = P("blk", split), P(split, None)
    return jax.shard_map(
        on_device,
        mesh=mesh,
        in_specs=(
            tokens, tokens, tokens, weights, tokens, tokens, tokens, weights, P("blk"),
            P("blk", None),
        ),
        out_specs=(tokens,) * 4,
        check_vma=False,
    )
```

```python
import functools

import jax
import jax.numpy as jnp
from jax import lax
from jax.experimental import pallas as pl
from jax.experimental.pallas import tpu as pltpu
from jax.sharding import PartitionSpec as P

HD = 128
BS = 64
SCALE = HD ** (-0.5)
LOG2E = 1.4426950408889634
MASKED = -1e30
VMEM_LIMIT = 56 * 1024 * 1024

NT = (((1,), (1,)), ((), ()))
TN = (((0,), (0,)), ((), ()))


def dot(a, b, dims=(((1,), (0,)), ((), ()))):
    return lax.dot_general(a, b, dims, preferred_element_type=jnp.float32)


def visible(key_pos, query_pos, first_count):
    low = jnp.where(query_pos < first_count, 0, first_count)
    return (key_pos <= query_pos) & (key_pos >= low)


def teacher_kernel(tile, info_ref, q_ref, k_ref, v_ref, o_ref):
    offset, first_count = info_ref[0], info_ref[1]
    q_tile = q_ref.shape[0]
    q_start = offset + pl.program_id(1) * q_tile
    q_end = q_start + q_tile
    queries = q_ref[...]

    def step(index, carried, masked):
        largest, total, acc = carried
        rows = pl.ds(pl.multiple_of(index * tile, tile), tile)
        scores = dot(k_ref[rows, :], queries, NT)
        if masked:
            key_pos = index * tile + lax.broadcasted_iota(jnp.int32, scores.shape, 0)
            query_pos = q_start + lax.broadcasted_iota(jnp.int32, (1, q_tile), 1)
            scores = jnp.where(visible(key_pos, query_pos, first_count), scores, MASKED)
        new = jnp.maximum(largest, jnp.max(scores, axis=0, keepdims=True))
        weights = jnp.exp2((scores - new) * (SCALE * LOG2E))
        if masked:
            weights = jnp.where(scores > 0.5 * MASKED, weights, 0.0)
        factor = jnp.exp2((largest - new) * (SCALE * LOG2E))
        total = total * factor + jnp.sum(weights, axis=0, keepdims=True)
        acc = acc * factor + dot(v_ref[rows, :], weights.astype(jnp.bfloat16), TN)
        return new, total, acc

    first = jnp.where(q_start >= first_count, first_count // tile, 0)
    last = (q_end + tile - 1) // tile
    straddles = first_count < q_end

    def general(index, carried):
        low, high = index * tile, (index + 1) * tile
        need = (high > q_start) | ((low < first_count) & straddles)
        return lax.cond(
            need,
            lambda c: step(index, c, True),
            lambda c: step(index, c, False),
            carried,
        )

    carried = (
        jnp.full((1, q_tile), MASKED, jnp.float32),
        jnp.zeros((1, q_tile), jnp.float32),
        jnp.zeros((HD, q_tile), jnp.float32),
    )
    _, total, acc = lax.fori_loop(first, last, general, carried)
    o_ref[...] = (acc / total).T.astype(jnp.bfloat16)


def teacher(queries, keys, values, heads, columns, offset, first_count):
    rows, tokens = queries.shape[0], keys.shape[0]
    width = heads * HD
    step, (q_at, k_at, v_at) = columns
    tile = 512
    info = jnp.stack([offset, first_count]).astype(jnp.int32)
    return pl.pallas_call(
        functools.partial(teacher_kernel, tile),
        grid_spec=pltpu.PrefetchScalarGridSpec(
            num_scalar_prefetch=1,
            grid=(heads, rows // tile),
            in_specs=[
                pl.BlockSpec((tile, HD), lambda h, i, s: (i, step * h + q_at)),
                pl.BlockSpec((tokens, HD), lambda h, i, s: (0, step * h + k_at)),
                pl.BlockSpec((tokens, HD), lambda h, i, s: (0, step * h + v_at)),
            ],
            out_specs=pl.BlockSpec((tile, HD), lambda h, i, s: (i, h)),
        ),
        out_shape=jax.ShapeDtypeStruct((rows, width), jnp.bfloat16),
        compiler_params=pltpu.CompilerParams(vmem_limit_bytes=VMEM_LIMIT),
        cost_estimate=pl.CostEstimate(
            flops=2 * rows * tokens * width, bytes_accessed=8 * tokens * width, transcendentals=0
        ),
    )(info, queries, keys, values)


def spread(ref, scratch, heads):
    for h in range(heads):
        cols = slice(h * HD, (h + 1) * HD)
        scratch[h * BS : (h + 1) * BS, cols] = ref[:, cols].astype(scratch.dtype)


def student_weights(sel_ref, place_ref, info_ref, q_wide, k_all, v_all, k_sel, v_sel, pos, heads):
    block = pl.program_id(0)
    count = sel_ref.shape[1]
    offset, first_count = info_ref[0], info_ref[1]
    within = lax.broadcasted_iota(jnp.int32, (BS, 1), 0)
    for e in range(count):
        chosen = sel_ref[block, e]
        source = pl.ds(pl.multiple_of(place_ref[block, e] * BS, BS), BS)
        k_sel[e * BS : (e + 1) * BS, :] = k_all[source, :]
        v_sel[e * BS : (e + 1) * BS, :] = v_all[source, :]
        pos[e * BS : (e + 1) * BS, :] = jnp.broadcast_to(chosen * BS + within, (BS, heads * BS))
    lane = lax.broadcasted_iota(jnp.int32, (1, heads * BS), 1)
    query_pos = offset + block * BS + lax.rem(lane, BS)
    scores = dot(k_sel[...], q_wide[...], NT)
    allowed = visible(pos[...], query_pos, first_count)
    scores = jnp.where(allowed, scores, MASKED)
    largest = jnp.max(scores, axis=0, keepdims=True)
    weights = jnp.exp2((scores - largest) * (SCALE * LOG2E))
    weights = jnp.where(allowed, weights, 0.0)
    return weights, jnp.sum(weights, axis=0, keepdims=True)


def forward_kernel(heads, sel_ref, place_ref, info_ref, q_ref, k_all, v_all, o_ref, q_wide, k_sel, v_sel, pos):
    @pl.when(pl.program_id(0) == 0)
    def _():
        q_wide[...] = jnp.zeros_like(q_wide)

    spread(q_ref, q_wide, heads)
    weights, total = student_weights(
        sel_ref, place_ref, info_ref, q_wide, k_all, v_all, k_sel, v_sel, pos, heads
    )
    weights = (weights / total).astype(jnp.bfloat16)
    blended = dot(weights, v_sel[...], TN)
    for h in range(heads):
        cols = slice(h * HD, (h + 1) * HD)
        o_ref[:, cols] = blended[h * BS : (h + 1) * BS, cols].astype(jnp.bfloat16)


def backward_kernel(
    heads, cycle, sel_ref, place_ref, info_ref, q_ref, g_ref, k_all, v_all, dq_ref, *rest
):
    own_ref, far_refs = rest[0], rest[1:cycle]
    dk_sum, dv_sum, q_wide, g_wide, k_sel, v_sel, pos = rest[cycle:]
    block = pl.program_id(0)

    @pl.when(block == 0)
    def _():
        q_wide[...] = jnp.zeros_like(q_wide)
        g_wide[...] = jnp.zeros_like(g_wide)
        dk_sum[...] = jnp.zeros_like(dk_sum)
        dv_sum[...] = jnp.zeros_like(dv_sum)

    spread(q_ref, q_wide, heads)
    spread(g_ref, g_wide, heads)
    weights, total = student_weights(
        sel_ref, place_ref, info_ref, q_wide, k_all, v_all, k_sel, v_sel, pos, heads
    )
    weights = weights / total
    weight_grad = dot(v_sel[...], g_wide[...], NT)
    row_dots = jnp.sum(weights * weight_grad, axis=0, keepdims=True)
    score_grad = (weights * (weight_grad - row_dots) * SCALE).astype(jnp.bfloat16)
    query_grad = dot(score_grad, k_sel[...], TN)
    for h in range(heads):
        cols = slice(h * HD, (h + 1) * HD)
        dq_ref[:, cols] = query_grad[h * BS : (h + 1) * BS, cols]
    key_grad = dot(score_grad, q_wide[...])
    value_grad = dot(weights.astype(jnp.bfloat16), g_wide[...])
    for e in range(sel_ref.shape[1]):
        target = pl.ds(pl.multiple_of(place_ref[block, e] * BS, BS), BS)
        dk_sum[target, :] += key_grad[e * BS : (e + 1) * BS, :]
        dv_sum[target, :] += value_grad[e * BS : (e + 1) * BS, :]

    @pl.when(block == pl.num_programs(0) - 1)
    def _():
        rows = own_ref.shape[1]
        own_ref[0] = dk_sum[:rows, :]
        own_ref[1] = dv_sum[:rows, :]
        for d in range(1, cycle):
            far_refs[d - 1][0] = dk_sum[d * rows : (d + 1) * rows, :].astype(jnp.bfloat16)
            far_refs[d - 1][1] = dv_sum[d * rows : (d + 1) * rows, :].astype(jnp.bfloat16)


def student_scratch(heads, keys, wides):
    width = heads * HD
    return [pltpu.VMEM((heads * BS, width), jnp.bfloat16)] * wides + [
        pltpu.VMEM((keys, width), jnp.bfloat16),
        pltpu.VMEM((keys, width), jnp.bfloat16),
        pltpu.VMEM((keys, heads * BS), jnp.int32),
    ]


def student_forward(tables, queries, keys, values):
    rows, width = queries.shape
    tokens = keys.shape[0]
    heads = width // HD
    row_block = pl.BlockSpec((BS, width), lambda b, *_: (b, 0))
    whole = pl.BlockSpec((tokens, width), lambda b, *_: (0, 0))
    return pl.pallas_call(
        functools.partial(forward_kernel, heads),
        grid_spec=pltpu.PrefetchScalarGridSpec(
            num_scalar_prefetch=3,
            grid=(rows // BS,),
            in_specs=[row_block, whole, whole],
            out_specs=row_block,
            scratch_shapes=student_scratch(heads, tables[0].shape[1] * BS, 1),
        ),
        out_shape=jax.ShapeDtypeStruct((rows, width), jnp.bfloat16),
        compiler_params=pltpu.CompilerParams(vmem_limit_bytes=VMEM_LIMIT),
        cost_estimate=pl.CostEstimate(
            flops=16 * rows * tokens * width, bytes_accessed=4 * tokens * width, transcendentals=0
        ),
    )(*tables, queries, keys, values)


def student_backward(tables, queries, grads, keys, values):
    rows, width = queries.shape
    tokens = keys.shape[0]
    cycle = tokens // rows
    heads = width // HD
    row_block = pl.BlockSpec((BS, width), lambda b, *_: (b, 0))
    whole = pl.BlockSpec((tokens, width), lambda b, *_: (0, 0))
    pair = pl.BlockSpec((2, rows, width), lambda b, *_: (0, 0, 0))
    return pl.pallas_call(
        functools.partial(backward_kernel, heads, cycle),
        grid_spec=pltpu.PrefetchScalarGridSpec(
            num_scalar_prefetch=3,
            grid=(rows // BS,),
            in_specs=[row_block, row_block, whole, whole],
            out_specs=[row_block] + [pair] * cycle,
            scratch_shapes=[pltpu.VMEM((tokens, width), jnp.float32)] * 2
            + student_scratch(heads, tables[0].shape[1] * BS, 2),
        ),
        out_shape=[
            jax.ShapeDtypeStruct((rows, width), jnp.float32),
            jax.ShapeDtypeStruct((2, rows, width), jnp.float32),
        ]
        + [jax.ShapeDtypeStruct((2, rows, width), jnp.bfloat16)] * (cycle - 1),
        compiler_params=pltpu.CompilerParams(vmem_limit_bytes=VMEM_LIMIT),
        cost_estimate=pl.CostEstimate(
            flops=32 * rows * tokens * width, bytes_accessed=8 * tokens * width, transcendentals=0
        ),
    )(*tables, queries, grads, keys, values)


def project_kernel(s_attn, t_attn, s_out, t_out, o_ref):
    o_ref[0] = (dot(s_attn[...], s_out[...]) - dot(t_attn[...], t_out[...])).astype(jnp.bfloat16)


def project(s_attn, t_attn, s_out, t_out, groups):
    rows = s_attn.shape[0]
    model = s_out.shape[1]
    tile = model // groups
    return pl.pallas_call(
        project_kernel,
        grid=(groups,),
        in_specs=[
            pl.BlockSpec(s_attn.shape, lambda j: (0, 0)),
            pl.BlockSpec(t_attn.shape, lambda j: (0, 0)),
            pl.BlockSpec((s_attn.shape[1], tile), lambda j: (0, j)),
            pl.BlockSpec((t_attn.shape[1], tile), lambda j: (0, j)),
        ],
        out_specs=pl.BlockSpec((1, rows, tile), lambda j: (j, 0, 0)),
        out_shape=jax.ShapeDtypeStruct((groups, rows, tile), jnp.bfloat16),
        compiler_params=pltpu.CompilerParams(vmem_limit_bytes=VMEM_LIMIT),
    )(s_attn, t_attn, s_out, t_out)


def project_grads_kernel(t_width, s_attn, t_attn, mix, o_ref):
    pieces, rows, width = mix.shape
    columns = mix[...].reshape(pieces * rows, width)
    o_ref[0] = (
        dot(s_attn[...], columns[:, t_width:], NT) - dot(t_attn[...], columns[:, :t_width], NT)
    ).astype(jnp.bfloat16)


def project_grads(s_attn, t_attn, mix, groups):
    rows = s_attn.shape[0]
    pieces, depth, width = mix.shape
    tile = depth // groups
    return pl.pallas_call(
        functools.partial(project_grads_kernel, t_attn.shape[1]),
        grid=(groups,),
        in_specs=[
            pl.BlockSpec(s_attn.shape, lambda j: (0, 0)),
            pl.BlockSpec(t_attn.shape, lambda j: (0, 0)),
            pl.BlockSpec((pieces, tile, width), lambda j: (0, j, 0)),
        ],
        out_specs=pl.BlockSpec((1, rows, pieces * tile), lambda j: (j, 0, 0)),
        out_shape=jax.ShapeDtypeStruct((groups, rows, pieces * tile), jnp.bfloat16),
        compiler_params=pltpu.CompilerParams(vmem_limit_bytes=VMEM_LIMIT),
    )(s_attn, t_attn, mix)


def from_earlier(rows, distance):
    route = [(i - distance, i) for i in range(distance, lax.axis_size("blk"))]
    return lax.ppermute(rows, "blk", route)


MESH = pl.DeviceIdType.MESH


def greet(blk, grp, cycle, cores):
    barrier = pltpu.get_barrier_semaphore()
    for d in range(cycle):
        for e in range(cores):
            if d or e:
                pl.semaphore_signal(
                    barrier,
                    inc=1,
                    device_id={"blk": lax.rem(blk + d, cycle), "grp": lax.rem(grp + e, cores)},
                    device_id_type=MESH,
                )
    pl.semaphore_wait(barrier, cycle * cores - 1)


def send(src, dst, send_sem, recv_sem, blk, grp):
    return pltpu.make_async_remote_copy(
        src_ref=src,
        dst_ref=dst,
        send_sem=send_sem,
        recv_sem=recv_sem,
        device_id={"blk": blk, "grp": grp},
        device_id_type=MESH,
    )


def arrive_kernel(
    cycle, cores, tq, tk, tv, sq, sk, sv, ints,
    oq, ok, ov, pq, pk, pv, oints,
    t_stage, s_stage, local, s_send, s_recv, x_send, x_recv, t_send, t_recv, i_send, i_recv,
):
    blk, grp = lax.axis_index("blk"), lax.axis_index("grp")
    rows = tq.shape[0]
    half = rows // cores
    share = cycle // cores
    owner = blk // share
    greet(blk, grp, cycle, cores)

    def student_copy(t, j, e):
        src = (sq, sk, sv)[t].at[pl.ds(e * half, half), pl.ds(j * HD, HD)]
        dst = (pq.at[blk], pk.at[e, blk], pv.at[e, blk])[t]
        return src, dst

    def student_send(t, j, e):
        return send(
            *student_copy(t, j, e), s_send.at[t, j, e], s_recv.at[t, blk], grp * share + j, e
        )

    pieces = [(t, j, e) for t in (1, 2, 0) for j in range(share) for e in range(cores)]
    for t, j, e in pieces:
        mine = (grp * share + j == blk) & (grp == e)

        @pl.when(jnp.logical_not(mine))
        def _():
            student_send(t, j, e).start()

    int_copies = [
        send(ints, oints.at[blk], i_send.at[d - 1], i_recv.at[d - 1], lax.rem(blk + d, cycle), grp)
        for d in range(1, cycle)
    ]
    for copy in int_copies:
        copy.start()
    oints[blk] = ints[...]

    t_copies = []
    for t, (src, dst) in enumerate(((tk, ok), (tv, ov), (tq, oq))):
        for d in range(1, cycle):
            dest = lax.rem(blk + d, cycle)
            columns = pl.ds(pl.multiple_of(dest * HD, HD), HD)
            t_copies.append(
                send(
                    src.at[:, columns], dst.at[blk], t_send.at[t, d - 1], t_recv.at[t, d - 1], dest, grp
                )
            )
    for copy in t_copies:
        copy.start()

    columns = pl.ds(pl.multiple_of(blk * HD, HD), HD)
    for t, (src, dst) in enumerate(((tk, ok), (tv, ov), (tq, oq))):
        pltpu.make_async_copy(src.at[:, columns], t_stage.at[t], local.at[t]).start()
    for t, (src, dst) in enumerate(((tk, ok), (tv, ov), (tq, oq))):
        pltpu.make_async_copy(src.at[:, columns], t_stage.at[t], local.at[t]).wait()
        pltpu.make_async_copy(t_stage.at[t], dst.at[blk], local.at[t]).start()
    for t, (src, dst) in enumerate(((tk, ok), (tv, ov), (tq, oq))):
        pltpu.make_async_copy(t_stage.at[t], dst.at[blk], local.at[t]).wait()

    for t, j, e in pieces:
        mine = (grp * share + j == blk) & (grp == e)

        @pl.when(mine)
        def _():
            src, dst = student_copy(t, j, e)
            inward = pltpu.make_async_copy(src, s_stage, local.at[0])
            inward.start()
            inward.wait()
            outward = pltpu.make_async_copy(s_stage, dst, local.at[0])
            outward.start()
            outward.wait()

    other = lax.rem(grp + 1, cores)

    def arrival(t, s):
        dst = (pq.at[s], pk.at[grp, s], pv.at[grp, s])[t]
        return send(dst, dst, s_send.at[t, 0, 0], s_recv.at[t, s], other, other)

    def cross(t, s):
        ref = (None, pk, pv)[t].at[grp, s]
        return send(ref, ref, x_send.at[t - 1, s], x_recv.at[t - 1, s], blk, other)

    for t in (1, 2, 0):
        for s in range(cycle):
            remote = jnp.logical_not((s == blk) & (owner == grp))

            @pl.when(remote)
            def _():
                arrival(t, s).wait_recv()

            if t:
                cross(t, s).start()

    for t in (1, 2):
        for s in range(cycle):
            cross(t, s).wait()
    for copy in int_copies + t_copies:
        copy.wait()
    for t, j, e in pieces:
        mine = (grp * share + j == blk) & (grp == e)

        @pl.when(jnp.logical_not(mine))
        def _():
            student_send(t, j, e).wait_send()


def arrive(t_query, t_key, t_value, s_query, s_key, s_value, ints, cycle, cores):
    rows = t_query.shape[0]
    half = rows // cores
    share = cycle // cores
    kind = t_query.dtype
    any_space = pl.BlockSpec(memory_space=pl.ANY)
    vmem = pl.BlockSpec(memory_space=pltpu.VMEM)
    dma = pltpu.SemaphoreType.DMA
    return pl.pallas_call(
        functools.partial(arrive_kernel, cycle, cores),
        in_specs=[any_space] * 6 + [vmem],
        out_specs=[any_space] * 6 + [vmem],
        out_shape=[jax.ShapeDtypeStruct((cycle, rows, HD), kind)] * 3
        + [jax.ShapeDtypeStruct((cycle, half, HD), kind)]
        + [jax.ShapeDtypeStruct((cores, cycle, half, HD), kind)] * 2
        + [jax.ShapeDtypeStruct((cycle,) + ints.shape, ints.dtype)],
        scratch_shapes=[
            pltpu.VMEM((3, rows, HD), kind),
            pltpu.VMEM((half, HD), kind),
            dma((3,)),
            dma((3, share, cores)),
            dma((3, cycle)),
            dma((2, cycle)),
            dma((2, cycle)),
            dma((3, cycle - 1)),
            dma((3, cycle - 1)),
            dma((cycle - 1,)),
            dma((cycle - 1,)),
        ],
        compiler_params=pltpu.CompilerParams(
            collective_id=0, has_side_effects=True, vmem_limit_bytes=VMEM_LIMIT
        ),
        cost_estimate=pl.CostEstimate(
            flops=0, bytes_accessed=64 * rows * HD * 2 * cycle, transcendentals=0
        ),
    )(t_query, t_key, t_value, s_query, s_key, s_value, ints)


def depart_kernel(cycle, cores, dq, own, far, out, got, mine, x_send, x_recv, d_send, d_recv):
    blk, grp = lax.axis_index("blk"), lax.axis_index("grp")
    half = dq.shape[1]
    share = cycle // cores
    owner, slot = blk // share, lax.rem(blk, share)
    other = lax.rem(grp + 1, cores)
    greet(blk, grp, cycle, cores)

    def target(t, j, e):
        rows = pl.ds(pl.multiple_of(e * half, half), half)
        return out.at[t, rows, pl.ds(pl.multiple_of(j * HD, HD), HD)]

    def source(t, s):
        return dq.at[s] if t == 0 else mine.at[t - 1, s]

    def piece(t, s):
        return send(
            source(t, s), target(t, slot, grp), d_send.at[t, s], d_recv.at[t, slot, grp], s, owner
        )

    def local(s):
        return (s == blk) & (owner == grp)

    def emit(t, s):
        @pl.when(jnp.logical_not(local(s)))
        def _():
            piece(t, s).start()

        @pl.when(local(s))
        def _():
            target(t, slot, grp)[...] = source(t, s)[...]

    crossing = [
        send(far.at[t], got.at[t], x_send.at[t], x_recv.at[t], blk, other) for t in range(2)
    ]
    for copy in crossing:
        copy.start()
    for s in range(cycle):
        emit(0, s)
    for t in range(2):
        crossing[t].wait_recv()
        for s in range(cycle):
            mine[t, s] = (own[t, s] + got[t, s].astype(jnp.float32)).astype(jnp.bfloat16)
        for s in range(cycle):
            emit(t + 1, s)
    for copy in crossing:
        copy.wait_send()
    for t in range(3):
        for j in range(share):
            for e in range(cores):
                ours = (grp * share + j == blk) & (grp == e)

                @pl.when(jnp.logical_not(ours))
                def _():
                    ref = target(t, j, e)
                    send(ref, ref, d_send.at[t, 0], d_recv.at[t, j, e], blk, other).wait_recv()

    for t in range(3):
        for s in range(cycle):
            @pl.when(jnp.logical_not(local(s)))
            def _():
                piece(t, s).wait_send()


def depart(dq, own, far, cycle, cores):
    half = dq.shape[1]
    share = cycle // cores
    vmem = pl.BlockSpec(memory_space=pltpu.VMEM)
    dma = pltpu.SemaphoreType.DMA
    return pl.pallas_call(
        functools.partial(depart_kernel, cycle, cores),
        in_specs=[vmem] * 3,
        out_specs=vmem,
        out_shape=jax.ShapeDtypeStruct((3, cores * half, share * HD), jnp.bfloat16),
        scratch_shapes=[
            pltpu.VMEM((2, cycle, half, HD), jnp.bfloat16),
            pltpu.VMEM((2, cycle, half, HD), jnp.bfloat16),
            dma((2,)),
            dma((2,)),
            dma((3, cycle)),
            dma((3, share, cores)),
        ],
        compiler_params=pltpu.CompilerParams(
            collective_id=1, has_side_effects=True, vmem_limit_bytes=VMEM_LIMIT
        ),
    )(dq, own, far)


def pair_weights(sel_ref, place_ref, info_ref, per_blk, q_wide, k_all, v_all, k_sel, v_sel):
    pair = pl.program_id(0)
    count = sel_ref.shape[1]
    first_count, grp = info_ref[0], info_ref[1]
    mine = per_blk // info_ref[2]

    def query_block(index):
        return (index // mine) * per_blk + grp * mine + lax.rem(index, mine)

    for e in range(count):
        for h in range(2):
            source = pl.ds(pl.multiple_of(place_ref[2 * pair + h, e] * BS, BS), BS)
            cols = slice(h * HD, (h + 1) * HD)
            k_sel[e * BS : (e + 1) * BS, cols] = k_all[source, :]
            v_sel[e * BS : (e + 1) * BS, cols] = v_all[source, :]
    within = lax.broadcasted_iota(jnp.int32, (BS, 1), 0)
    lane = lax.broadcasted_iota(jnp.int32, (1, 2 * BS), 1)
    second = lane >= BS
    query_pos = (
        jnp.where(second, query_block(2 * pair + 1), query_block(2 * pair)) * BS + lax.rem(lane, BS)
    )
    low = jnp.where(query_pos < first_count, 0, first_count)
    scores = dot(k_sel[...], q_wide[...], NT)
    allowed = []
    for e in range(count):
        base = jnp.where(second, sel_ref[2 * pair + 1, e], sel_ref[2 * pair, e]) * BS
        allowed.append((within <= query_pos - base) & (within >= low - base))
    scores = jnp.concatenate(
        [jnp.where(a, scores[e * BS : (e + 1) * BS], MASKED) for e, a in enumerate(allowed)]
    )
    largest = jnp.max(scores, axis=0, keepdims=True)
    weights = jnp.exp2((scores - largest) * (SCALE * LOG2E))
    weights = jnp.concatenate(
        [jnp.where(a, weights[e * BS : (e + 1) * BS], 0.0) for e, a in enumerate(allowed)]
    )
    return weights, jnp.sum(weights, axis=0, keepdims=True)


def spread_pair(ref, scratch):
    for h in range(2):
        scratch[h * BS : (h + 1) * BS, h * HD : (h + 1) * HD] = ref[h * BS : (h + 1) * BS, :].astype(
            scratch.dtype
        )


def pair_forward_kernel(
    per_blk, sel_ref, place_ref, info_ref, q_ref, k_all, v_all, o_ref, q_wide, k_sel, v_sel
):
    @pl.when(pl.program_id(0) == 0)
    def _():
        q_wide[...] = jnp.zeros_like(q_wide)

    spread_pair(q_ref, q_wide)
    weights, total = pair_weights(
        sel_ref, place_ref, info_ref, per_blk, q_wide, k_all, v_all, k_sel, v_sel
    )
    weights = (weights / total).astype(jnp.bfloat16)
    blended = dot(weights, v_sel[...], TN)
    for h in range(2):
        o_ref[h * BS : (h + 1) * BS, :] = blended[
            h * BS : (h + 1) * BS, h * HD : (h + 1) * HD
        ].astype(jnp.bfloat16)


def pair_backward_kernel(
    per_blk, sel_ref, place_ref, info_ref, q_ref, g_ref, k_all, v_all, dq_ref, own_ref, far_ref,
    dk_sum, dv_sum, q_wide, g_wide, k_sel, v_sel,
):
    pair = pl.program_id(0)

    @pl.when(pair == 0)
    def _():
        q_wide[...] = jnp.zeros_like(q_wide)
        g_wide[...] = jnp.zeros_like(g_wide)
        dk_sum[...] = jnp.zeros_like(dk_sum)
        dv_sum[...] = jnp.zeros_like(dv_sum)

    spread_pair(q_ref, q_wide)
    spread_pair(g_ref, g_wide)
    weights, total = pair_weights(
        sel_ref, place_ref, info_ref, per_blk, q_wide, k_all, v_all, k_sel, v_sel
    )
    weights = weights / total
    weight_grad = dot(v_sel[...], g_wide[...], NT)
    row_dots = jnp.sum(weights * weight_grad, axis=0, keepdims=True)
    score_grad = (weights * (weight_grad - row_dots) * SCALE).astype(jnp.bfloat16)
    query_grad = dot(score_grad, k_sel[...], TN)
    for h in range(2):
        dq_ref[h * BS : (h + 1) * BS, :] = query_grad[
            h * BS : (h + 1) * BS, h * HD : (h + 1) * HD
        ].astype(jnp.bfloat16)
    key_grad = dot(score_grad, q_wide[...])
    value_grad = dot(weights.astype(jnp.bfloat16), g_wide[...])
    for e in range(sel_ref.shape[1]):
        for h in range(2):
            target = pl.ds(pl.multiple_of(place_ref[2 * pair + h, e] * BS, BS), BS)
            cols = slice(h * HD, (h + 1) * HD)
            dk_sum[target, :] += key_grad[e * BS : (e + 1) * BS, cols]
            dv_sum[target, :] += value_grad[e * BS : (e + 1) * BS, cols]

    @pl.when(pair == pl.num_programs(0) - 1)
    def _():
        part = own_ref.shape[1]
        near = pl.ds(pl.multiple_of(info_ref[1] * part, part), part)
        away = pl.ds(pl.multiple_of((info_ref[2] - 1 - info_ref[1]) * part, part), part)
        own_ref[0] = dk_sum[near, :]
        own_ref[1] = dv_sum[near, :]
        far_ref[0] = dk_sum[away, :].astype(jnp.bfloat16)
        far_ref[1] = dv_sum[away, :].astype(jnp.bfloat16)


def pair_scratch(keys, wides):
    return [pltpu.VMEM((2 * BS, 2 * HD), jnp.bfloat16)] * wides + [
        pltpu.VMEM((keys, 2 * HD), jnp.bfloat16),
        pltpu.VMEM((keys, 2 * HD), jnp.bfloat16),
    ]


def pair_forward(per_blk, tables, queries, keys, values):
    rows, width = queries.shape
    tokens = keys.shape[0]
    row_block = pl.BlockSpec((2 * BS, width), lambda b, *_: (b, 0))
    whole = pl.BlockSpec((tokens, width), lambda b, *_: (0, 0))
    return pl.pallas_call(
        functools.partial(pair_forward_kernel, per_blk),
        grid_spec=pltpu.PrefetchScalarGridSpec(
            num_scalar_prefetch=3,
            grid=(rows // (2 * BS),),
            in_specs=[row_block, whole, whole],
            out_specs=row_block,
            scratch_shapes=pair_scratch(tables[0].shape[1] * BS, 1),
        ),
        out_shape=jax.ShapeDtypeStruct((rows, width), jnp.bfloat16),
        compiler_params=pltpu.CompilerParams(vmem_limit_bytes=VMEM_LIMIT),
        cost_estimate=pl.CostEstimate(
            flops=16 * rows * tokens * width, bytes_accessed=4 * tokens * width, transcendentals=0
        ),
    )(*tables, queries, keys, values)


def pair_backward(per_blk, cores, tables, queries, grads, keys, values):
    rows, width = queries.shape
    tokens = keys.shape[0]
    part = tokens // cores
    row_block = pl.BlockSpec((2 * BS, width), lambda b, *_: (b, 0))
    whole = pl.BlockSpec((tokens, width), lambda b, *_: (0, 0))
    both = pl.BlockSpec((2, part, width), lambda b, *_: (0, 0, 0))
    return pl.pallas_call(
        functools.partial(pair_backward_kernel, per_blk),
        grid_spec=pltpu.PrefetchScalarGridSpec(
            num_scalar_prefetch=3,
            grid=(rows // (2 * BS),),
            in_specs=[row_block, row_block, whole, whole],
            out_specs=[row_block, both, both],
            scratch_shapes=[pltpu.VMEM((tokens, width), jnp.float32)] * 2
            + pair_scratch(tables[0].shape[1] * BS, 2),
        ),
        out_shape=[
            jax.ShapeDtypeStruct((rows, width), jnp.bfloat16),
            jax.ShapeDtypeStruct((2, part, width), jnp.float32),
            jax.ShapeDtypeStruct((2, part, width), jnp.bfloat16),
        ],
        compiler_params=pltpu.CompilerParams(vmem_limit_bytes=VMEM_LIMIT),
        cost_estimate=pl.CostEstimate(
            flops=32 * rows * tokens * width, bytes_accessed=8 * tokens * width, transcendentals=0
        ),
    )(*tables, queries, grads, keys, values)


def combine_kernel(
    cycle, cores, line, chunks, kept, heads_t, heads_s, mix_hbm, t_hbm, s_hbm,
    g_out, m_out, terms,
    mix, t_w, s_w, t_attn, s_attn, g_own, g_far, g_got, g_line, m_own, m_far, m_got, m_line,
    total, g_done, w_sem, t_send, t_recv, t_local, s_send, s_recv, s_local,
    gx_send, gx_recv, gz_send, gz_recv, mx_send, mx_recv, mz_send, mz_recv, d_send, d_recv,
):
    blk, grp, pos = lax.axis_index("blk"), lax.axis_index("grp"), lax.axis_index("head")
    share = cycle // cores
    owner, slot = blk // share, lax.rem(blk, share)
    other = lax.rem(grp + 1, cores)
    step = t_attn.shape[0] // chunks
    per_half = chunks // cores

    loads = [
        pltpu.make_async_copy(src, dst, w_sem.at[n])
        for n, (src, dst) in enumerate(((mix_hbm, mix), (t_hbm, t_w), (s_hbm, s_w)))
    ]
    for load in loads:
        load.start()

    barrier = pltpu.get_barrier_semaphore()
    for d in range(cycle):
        for e in range(cores):
            if d or e:
                pl.semaphore_signal(
                    barrier,
                    inc=1,
                    device_id={"blk": lax.rem(blk + d, cycle), "grp": lax.rem(grp + e, cores)},
                    device_id_type=MESH,
                )
    for ahead, there in ((-1, pos > 0), (1, pos < line - 1)):
        @pl.when(there)
        def _():
            pl.semaphore_signal(
                barrier, inc=1, device_id={"head": pos + ahead}, device_id_type=MESH
            )

    ends = jnp.where(pos > 0, 1, 0) + jnp.where(pos < line - 1, 1, 0)
    pl.semaphore_wait(barrier, cycle * cores - 1 + ends)

    def t_copy(i, d):
        dest = lax.rem(blk + d, cycle)
        src = heads_t.at[dest, pl.ds(i * step, step), :]
        dst = t_attn.at[pl.ds(i * step, step), pl.ds(pl.multiple_of(blk * HD, HD), HD)]
        if d == 0:
            return pltpu.make_async_copy(src, dst, t_local.at[i])
        return send(src, dst, t_send.at[i, d - 1], t_recv.at[i, d - 1], dest, grp)

    def s_ends(r, s):
        rows = pl.ds(pl.multiple_of((grp * per_half + r) * step, step), step)
        dst = s_attn.at[rows, pl.ds(pl.multiple_of(slot * HD, HD), HD)]
        return heads_s.at[s, pl.ds(r * step, step), :], dst

    def s_copy(r, s):
        return send(
            *s_ends(r, s), s_send.at[r, s], s_recv.at[slot, grp * per_half + r], s, owner
        )

    def s_here(r, s):
        return pltpu.make_async_copy(*s_ends(r, s), s_local.at[r])

    for i in range(chunks):
        for d in range(cycle):
            t_copy(i, d).start()
        if i < per_half:
            for s in range(cycle):
                here = (s == blk) & (owner == grp)

                @pl.when(here)
                def _():
                    s_here(i, s).start()

                @pl.when(jnp.logical_not(here))
                def _():
                    s_copy(i, s).start()

    def await_inputs(i):
        for d in range(1, cycle):
            t_copy(i, d).wait_recv()
        t_copy(i, 0).wait()
        e, r = i // per_half, i % per_half
        for j in range(share):
            here = (grp * share + j == blk) & (grp == e)

            @pl.when(here)
            def _():
                s_here(r, grp * share + j).wait()

            @pl.when(jnp.logical_not(here))
            def _():
                ref = s_attn.at[pl.ds(i * step, step), pl.ds(j * HD, HD)]
                send(ref, ref, s_send.at[r, 0], s_recv.at[j, i], blk, other).wait_recv()

    t_width, s_width = t_attn.shape[1], s_attn.shape[1]

    def rows_of(i):
        rows = pl.ds(i * step, step)
        return t_attn[rows, :], s_attn[rows, :]

    def grad_term(i, group):
        t_rows, s_rows = rows_of(i)
        depth = mix.shape[1] // (line * cores)
        part = mix[:, pl.ds(pl.multiple_of(group * depth, depth), depth), :]
        part = part.reshape(mix.shape[0] * depth, mix.shape[2])
        value = dot(s_rows, part[:, t_width:], NT) - dot(t_rows, part[:, :t_width], NT)
        return value.astype(jnp.bfloat16)

    def out_term(i, group):
        t_rows, s_rows = rows_of(i)
        width = t_w.shape[1] // (line * cores)
        cols = pl.ds(pl.multiple_of(group * width, width), width)
        return (dot(s_rows, s_w[:, cols]) - dot(t_rows, t_w[:, cols])).astype(jnp.bfloat16)

    kinds = {
        "g": (grad_term, g_own, g_far, g_got, g_line, gx_send, gx_recv, gz_send, gz_recv),
        "m": (out_term, m_own, m_far, m_got, m_line, mx_send, mx_recv, mz_send, mz_recv),
    }

    def cross(kind, i):
        _, _, far, got, _, x_send, x_recv, _, _ = kinds[kind]
        return send(far.at[i], got.at[i], x_send.at[i], x_recv.at[i], blk, other)

    def hop(kind, i, way, dest, target):
        _, own, _, _, relay, _, _, z_send, z_recv = kinds[kind]
        return pltpu.make_async_remote_copy(
            src_ref=own.at[i, dest],
            dst_ref=relay.at[way, i, dest],
            send_sem=z_send.at[i, dest],
            recv_sem=z_recv.at[way, i, dest],
            device_id={"head": target},
            device_id_type=MESH,
        )

    def compute(kind, i):
        if kind == "g":
            await_inputs(i)
        if (kind, i) == ("g", 0):
            loads[0].wait()
        if (kind, i) == ("m", 0):
            loads[1].wait()
            loads[2].wait()
        term, own, far = kinds[kind][:3]

        def body(z, carry):
            far[i, z] = term(i, z * cores + other)
            own[i, z] = term(i, z * cores + grp)
            return carry

        lax.fori_loop(0, line, body, 0)
        cross(kind, i).start()

    def add(kind, i, dest, ref):
        own = kinds[kind][1]
        own[i, dest] = (
            own[i, dest].astype(jnp.float32) + ref[...].astype(jnp.float32)
        ).astype(jnp.bfloat16)

    def fold(kind, i):
        got = kinds[kind][3]
        cross(kind, i).wait_recv()

        def body(z, carry):
            add(kind, i, z, got.at[i, z])
            return carry

        lax.fori_loop(0, line, body, 0)

    def flow(kind, i, upward):
        way = jnp.where(upward, 0, 1)
        target = jnp.where(upward, pos + 1, pos - 1)
        count = jnp.where(upward, line - 1 - pos, pos)
        fed = jnp.where(upward, pos, line - 1 - pos) > 0
        relay = kinds[kind][4]

        def body(k, carry):
            dest = jnp.where(upward, line - 1 - k, k)

            @pl.when(fed)
            def _():
                hop(kind, i, way, dest, target).wait_recv()
                add(kind, i, dest, relay.at[way, i, dest])

            hop(kind, i, way, dest, target).start()
            return carry

        lax.fori_loop(0, count, body, 0)

    def final(kind, i):
        own, relay = kinds[kind][1], kinds[kind][4]
        width = own.shape[3]
        total[:, :width] = own[i, pos].astype(jnp.float32)
        for way, fed in ((0, pos > 0), (1, pos < line - 1)):
            @pl.when(fed)
            def _():
                hop(kind, i, way, pos, pos).wait_recv()
                total[:, :width] += relay[way, i, pos].astype(jnp.float32)

        if kind == "m":
            m_out[pl.ds(i * step, step), :] = total[...]
            return
        for j in range(share):
            g_done[i, j] = total[:, j * HD : (j + 1) * HD].astype(jnp.bfloat16)
            here = (grp * share + j == blk) & (grp == i // per_half)

            @pl.when(here)
            def _():
                g_out[blk, pl.ds(i % per_half * step, step), :] = g_done[i, j]

            @pl.when(jnp.logical_not(here))
            def _():
                deliver(i, j).start()

    def deliver(i, j):
        r = i % per_half
        return send(
            g_done.at[i, j],
            g_out.at[blk, pl.ds(r * step, step), :],
            d_send.at[i, j],
            d_recv.at[blk, r],
            grp * share + j,
            i // per_half,
        )

    low = pos < line // 2
    items = [("g", i) for i in range(chunks)] + [("m", i) for i in range(kept)]
    for k in range(len(items) + 3):
        if k < len(items):
            compute(*items[k])
        if k == len(items) and kept < chunks:
            if not kept:
                loads[1].wait()
                loads[2].wait()

            def body(group, carry):
                for i in range(kept, chunks):
                    terms[group, pl.ds((i - kept) * step, step), :] = out_term(i, group)
                return carry

            lax.fori_loop(0, line * cores, body, 0)
        if 0 <= k - 1 < len(items):
            fold(*items[k - 1])
            flow(*items[k - 1], low)
        if 0 <= k - 2 < len(items):
            flow(*items[k - 2], jnp.logical_not(low))
        if 0 <= k - 3 < len(items):
            final(*items[k - 3])

    for s in range(cycle):
        here = (s == blk) & (owner == grp)

        @pl.when(jnp.logical_not(here))
        def _():
            for r in range(per_half):
                ref = g_out.at[s, pl.ds(r * step, step), :]
                send(ref, ref, d_send.at[0, 0], d_recv.at[s, r], other, other).wait_recv()

    for i in range(chunks):
        for d in range(1, cycle):
            t_copy(i, d).wait_send()
        if i < per_half:
            for s in range(cycle):
                @pl.when(jnp.logical_not((s == blk) & (owner == grp)))
                def _():
                    s_copy(i, s).wait_send()
        for j in range(share):
            @pl.when(jnp.logical_not((grp * share + j == blk) & (grp == i // per_half)))
            def _():
                deliver(i, j).wait_send()

    for kind, i in items:
        cross(kind, i).wait_send()
        for dest in range(line):
            @pl.when(dest != pos)
            def _():
                hop(kind, i, 0, dest, other).wait_send()


def combine(heads_t, heads_s, mix, t_out, s_out, cycle, cores, line, kept):
    rows = heads_t.shape[1]
    chunks = 2 * cores
    step = rows // chunks
    share = cycle // cores
    groups = line * cores
    wide = t_out.shape[1] // groups
    t_width, s_width = t_out.shape[0], s_out.shape[0]
    half = rows // cores
    kind = jnp.bfloat16
    any_space = pl.BlockSpec(memory_space=pl.ANY)
    vmem = pl.BlockSpec(memory_space=pltpu.VMEM)
    dma = pltpu.SemaphoreType.DMA
    held = max(kept, 1)
    rest = max(chunks - kept, 1)

    def lines(n, width):
        block = (n, line, step, width)
        return [pltpu.VMEM(block, kind)] * 3 + [pltpu.VMEM((2,) + block, kind)]

    def line_sems(n):
        return [dma((n,)), dma((n,)), dma((n, line)), dma((2, n, line))]

    return pl.pallas_call(
        functools.partial(combine_kernel, cycle, cores, line, chunks, kept),
        in_specs=[any_space] * 5,
        out_specs=[vmem] * 3,
        out_shape=[
            jax.ShapeDtypeStruct((cycle, half, HD), kind),
            jax.ShapeDtypeStruct((held * step, wide), jnp.float32),
            jax.ShapeDtypeStruct((groups, rest * step, wide), kind),
        ],
        scratch_shapes=[
            pltpu.VMEM(mix.shape, kind),
            pltpu.VMEM(t_out.shape, kind),
            pltpu.VMEM(s_out.shape, kind),
            pltpu.VMEM((rows, t_width), kind),
            pltpu.VMEM((rows, s_width), kind),
        ]
        + lines(chunks, s_width)
        + lines(held, wide)
        + [
            pltpu.VMEM((step, wide), jnp.float32),
            pltpu.VMEM((chunks, share, step, HD), kind),
            dma((3,)),
            dma((chunks, cycle - 1)),
            dma((chunks, cycle - 1)),
            dma((chunks,)),
            dma((chunks // cores, cycle)),
            dma((share, chunks)),
            dma((chunks // cores,)),
        ]
        + line_sems(chunks)
        + line_sems(held)
        + [dma((chunks, share)), dma((cycle, chunks // cores))],
        compiler_params=pltpu.CompilerParams(
            collective_id=2, has_side_effects=True, vmem_limit_bytes=VMEM_LIMIT
        ),
        cost_estimate=pl.CostEstimate(
            flops=0, bytes_accessed=64 * rows * wide * groups, transcendentals=0
        ),
    )(heads_t, heads_s, mix, t_out, s_out)


def heads_on_chips(
    t_query, t_key, t_value, t_out, s_query, s_key, s_value, s_out, segments, selection
):
    rows = t_query.shape[0]
    cycle, cores = lax.axis_size("blk"), lax.axis_size("grp")
    split = ("head", "grp")
    groups = lax.axis_size("head") * cores
    blk, grp = lax.axis_index("blk"), lax.axis_index("grp")
    half = rows // cores
    share = cycle // cores
    per_blk = rows // BS
    mine = per_blk // cores
    picks = selection.shape[1]

    piece = s_out.shape[0] // cycle
    s_rows = lax.dynamic_slice_in_dim(s_out, blk * piece, piece, 0)
    s_rows = lax.all_gather(s_rows, split, axis=0, tiled=True)

    lanes = 128
    ints = jnp.concatenate(
        [segments.reshape(rows // lanes, lanes), jnp.pad(selection, ((0, 0), (0, lanes - picks)))]
    )
    tq, tk, tv, pq, pk, pv, ints = arrive(
        t_query, t_key, t_value, s_query, s_key, s_value, ints, cycle, cores
    )
    s_rows, tq = lax.optimization_barrier((s_rows, tq))
    seg_rows = rows // lanes
    first_count = jnp.sum((ints[:, :seg_rows] == 0).astype(jnp.int32))
    info = jnp.stack([first_count, grp, jnp.int32(cores)]).astype(jnp.int32)
    chosen = lax.dynamic_slice_in_dim(ints[:, seg_rows:, :picks], grp * mine, mine, 1)
    chosen = chosen.reshape(cycle * mine, picks)
    at = chosen % per_blk
    place = ((at // mine) * cycle + chosen // per_blk) * mine + at % mine
    tables = (chosen, place, info)
    pq = pq.reshape(cycle * half, HD)
    pk, pv = pk.reshape(cycle * rows, HD), pv.reshape(cycle * rows, HD)

    blended = pair_forward(per_blk, tables, pq, pk, pv)
    tables, blended, tq = lax.optimization_barrier((tables, blended, tq))

    mix = jnp.concatenate([dot(s_rows, t_out, NT), dot(s_rows, s_out, NT)], axis=1)
    mix = lax.all_gather(mix.astype(jnp.bfloat16), "blk")

    whole = [x.reshape(cycle * rows, HD) for x in (tq, tk, tv)]
    whole_heads = teacher(*whole, 1, (1, (0, 0, 0)), jnp.int32(0), first_count)

    kept = 2
    grads, near, terms = combine(
        whole_heads.reshape(cycle, rows, HD), blended.reshape(cycle, half, HD), mix,
        t_out, s_out, cycle, cores, groups // cores, kept,
    )
    rest = lax.psum_scatter(terms, split, scatter_dimension=0, tiled=False)
    grads = grads.reshape(cycle * half, HD)
    dq, own, far = pair_backward(per_blk, cores, tables, pq, grads, pk, pv)
    out = depart(
        dq.reshape(cycle, half, HD),
        own.reshape(2, cycle, half, HD),
        far.reshape(2, cycle, half, HD),
        cycle,
        cores,
    ).astype(jnp.float32)
    mismatch = jnp.concatenate([near, rest.astype(jnp.float32)])
    return (mismatch, out[0], out[1], out[2])


def on_device(t_query, t_key, t_value, t_out, s_query, s_key, s_value, s_out, segments, selection):
    row_count = t_query.shape[0]
    heads = t_query.shape[1] // HD
    cycle = lax.axis_size("blk")
    split = ("head", "grp")
    groups = lax.axis_size("head") * lax.axis_size("grp")
    cores = lax.axis_size("grp")
    if cores == 2 and heads == cycle and s_query.shape[1] // HD * cores == cycle:
        return heads_on_chips(
            t_query, t_key, t_value, t_out, s_query, s_key, s_value, s_out, segments, selection
        )
    my_index = lax.axis_index("blk")
    first_row = my_index * row_count
    shard_blocks = row_count // BS

    count = jnp.sum((segments == 0).astype(jnp.int32)).reshape(1)
    first_count = count
    for distance in range(1, cycle):
        route = [(i, (i + distance) % cycle) for i in range(cycle)]
        first_count = first_count + lax.ppermute(count, "blk", route)
    first_count = first_count[0]
    info = jnp.stack([first_row, first_count]).astype(jnp.int32)

    piece = s_out.shape[0] // cycle
    s_rows = lax.dynamic_slice_in_dim(s_out, my_index * piece, piece, 0)
    s_rows = lax.all_gather(s_rows, split, axis=0, tiled=True)
    mix = jnp.concatenate([dot(s_rows, t_out, NT), dot(s_rows, s_out, NT)], axis=1)
    mix = lax.all_gather(mix.astype(jnp.bfloat16), "blk")

    if heads % cycle == 0:
        packed = jnp.concatenate(
            [rows.reshape(row_count, heads, HD) for rows in (t_query, t_key, t_value)], axis=2
        ).reshape(row_count, 3 * heads * HD)
        packed = lax.all_to_all(packed, "blk", split_axis=1, concat_axis=0, tiled=True)
        packed, s_key, s_value = lax.optimization_barrier((packed, s_key, s_value))
        whole_heads = teacher(
            packed, packed, packed, heads // cycle, (3, (0, 1, 2)), jnp.int32(0), first_count
        )
        t_attn = lax.all_to_all(whole_heads, "blk", split_axis=0, concat_axis=1, tiled=True)
    else:
        t_attn = teacher(
            t_query,
            lax.all_gather(t_key, "blk", axis=0, tiled=True),
            lax.all_gather(t_value, "blk", axis=0, tiled=True),
            heads,
            (1, (0, 0, 0)),
            first_row,
            first_count,
        )

    key_stack = jnp.concatenate([s_key] + [from_earlier(s_key, d) for d in range(1, cycle)])
    value_stack = jnp.concatenate([s_value] + [from_earlier(s_value, d) for d in range(1, cycle)])
    place = (my_index - selection // shard_blocks) * shard_blocks + selection % shard_blocks
    tables = (selection, place, info)
    s_attn = student_forward(tables, s_query, key_stack, value_stack)

    grad_terms = project_grads(s_attn, t_attn, mix, groups)
    grads = lax.psum_scatter(grad_terms, split, scatter_dimension=0, tiled=False)
    terms = project(s_attn, t_attn, s_out, t_out, groups)
    terms, grads = lax.optimization_barrier((terms, grads))
    mismatch = lax.psum_scatter(terms, split, scatter_dimension=0, tiled=False)

    grad_query, own, *far = student_backward(
        tables, s_query, grads, key_stack, value_stack
    )
    for distance in range(1, cycle):
        route = [(i, i - distance) for i in range(distance, cycle)]
        own = own + lax.ppermute(far[distance - 1], "blk", route).astype(jnp.float32)
    return (mismatch.astype(jnp.float32), grad_query, own[0], own[1])


def solution(mesh):
    split = ("head", "grp")
    tokens, weights = P("blk", split), P(split, None)
    return jax.shard_map(
        on_device,
        mesh=mesh,
        in_specs=(
            tokens, tokens, tokens, weights, tokens, tokens, tokens, weights, P("blk"),
            P("blk", None),
        ),
        out_specs=(tokens,) * 4,
        check_vma=False,
    )
```

```python
import functools

import jax
import jax.numpy as jnp
from jax import lax
from jax.experimental import pallas as pl
from jax.experimental.pallas import tpu as pltpu
from jax.sharding import PartitionSpec as P

HD = 128
BS = 64
SCALE = HD ** (-0.5)
LOG2E = 1.4426950408889634
MASKED = -1e30
VMEM_LIMIT = 56 * 1024 * 1024

NT = (((1,), (1,)), ((), ()))
TN = (((0,), (0,)), ((), ()))


def dot(a, b, dims=(((1,), (0,)), ((), ()))):
    return lax.dot_general(a, b, dims, preferred_element_type=jnp.float32)


def visible(key_pos, query_pos, first_count):
    low = jnp.where(query_pos < first_count, 0, first_count)
    return (key_pos <= query_pos) & (key_pos >= low)


def teacher_kernel(tile, info_ref, q_ref, k_ref, v_ref, o_ref):
    offset, first_count = info_ref[0], info_ref[1]
    q_tile = q_ref.shape[0]
    q_start = offset + pl.program_id(1) * q_tile
    q_end = q_start + q_tile
    queries = q_ref[...]

    def step(index, carried, masked):
        largest, total, acc = carried
        rows = pl.ds(pl.multiple_of(index * tile, tile), tile)
        scores = dot(k_ref[rows, :], queries, NT)
        if masked:
            key_pos = index * tile + lax.broadcasted_iota(jnp.int32, scores.shape, 0)
            query_pos = q_start + lax.broadcasted_iota(jnp.int32, (1, q_tile), 1)
            scores = jnp.where(visible(key_pos, query_pos, first_count), scores, MASKED)
        new = jnp.maximum(largest, jnp.max(scores, axis=0, keepdims=True))
        weights = jnp.exp2((scores - new) * (SCALE * LOG2E))
        if masked:
            weights = jnp.where(scores > 0.5 * MASKED, weights, 0.0)
        factor = jnp.exp2((largest - new) * (SCALE * LOG2E))
        total = total * factor + jnp.sum(weights, axis=0, keepdims=True)
        acc = acc * factor + dot(v_ref[rows, :], weights.astype(jnp.bfloat16), TN)
        return new, total, acc

    first = jnp.where(q_start >= first_count, first_count // tile, 0)
    last = (q_end + tile - 1) // tile
    straddles = first_count < q_end

    def general(index, carried):
        low, high = index * tile, (index + 1) * tile
        need = (high > q_start) | ((low < first_count) & straddles)
        return lax.cond(
            need,
            lambda c: step(index, c, True),
            lambda c: step(index, c, False),
            carried,
        )

    carried = (
        jnp.full((1, q_tile), MASKED, jnp.float32),
        jnp.zeros((1, q_tile), jnp.float32),
        jnp.zeros((HD, q_tile), jnp.float32),
    )
    _, total, acc = lax.fori_loop(first, last, general, carried)
    o_ref[...] = (acc / total).T.astype(jnp.bfloat16)


def teacher(info, queries, keys, values, heads, columns):
    rows, tokens = queries.shape[0], keys.shape[0]
    width = heads * HD
    step, (q_at, k_at, v_at) = columns
    tile = 512
    return pl.pallas_call(
        functools.partial(teacher_kernel, tile),
        grid_spec=pltpu.PrefetchScalarGridSpec(
            num_scalar_prefetch=1,
            grid=(heads, rows // tile),
            in_specs=[
                pl.BlockSpec((tile, HD), lambda h, i, s: (i, step * h + q_at)),
                pl.BlockSpec((tokens, HD), lambda h, i, s: (0, step * h + k_at)),
                pl.BlockSpec((tokens, HD), lambda h, i, s: (0, step * h + v_at)),
            ],
            out_specs=pl.BlockSpec((tile, HD), lambda h, i, s: (i, h)),
        ),
        out_shape=jax.ShapeDtypeStruct((rows, width), jnp.bfloat16),
        compiler_params=pltpu.CompilerParams(vmem_limit_bytes=VMEM_LIMIT),
        cost_estimate=pl.CostEstimate(
            flops=2 * rows * tokens * width, bytes_accessed=8 * tokens * width, transcendentals=0
        ),
    )(info, queries, keys, values)


def spread(ref, scratch, heads):
    for h in range(heads):
        cols = slice(h * HD, (h + 1) * HD)
        scratch[h * BS : (h + 1) * BS, cols] = ref[:, cols].astype(scratch.dtype)


def student_weights(sel_ref, place_ref, info_ref, q_wide, k_all, v_all, k_sel, v_sel, pos, heads):
    block = pl.program_id(0)
    count = sel_ref.shape[1]
    offset, first_count = info_ref[0], info_ref[1]
    within = lax.broadcasted_iota(jnp.int32, (BS, 1), 0)
    for e in range(count):
        chosen = sel_ref[block, e]
        source = pl.ds(pl.multiple_of(place_ref[block, e] * BS, BS), BS)
        k_sel[e * BS : (e + 1) * BS, :] = k_all[source, :]
        v_sel[e * BS : (e + 1) * BS, :] = v_all[source, :]
        pos[e * BS : (e + 1) * BS, :] = jnp.broadcast_to(chosen * BS + within, (BS, heads * BS))
    lane = lax.broadcasted_iota(jnp.int32, (1, heads * BS), 1)
    query_pos = offset + block * BS + lax.rem(lane, BS)
    scores = dot(k_sel[...], q_wide[...], NT)
    allowed = visible(pos[...], query_pos, first_count)
    scores = jnp.where(allowed, scores, MASKED)
    largest = jnp.max(scores, axis=0, keepdims=True)
    weights = jnp.exp2((scores - largest) * (SCALE * LOG2E))
    weights = jnp.where(allowed, weights, 0.0)
    return weights, jnp.sum(weights, axis=0, keepdims=True)


def forward_kernel(heads, sel_ref, place_ref, info_ref, q_ref, k_all, v_all, o_ref, q_wide, k_sel, v_sel, pos):
    @pl.when(pl.program_id(0) == 0)
    def _():
        q_wide[...] = jnp.zeros_like(q_wide)

    spread(q_ref, q_wide, heads)
    weights, total = student_weights(
        sel_ref, place_ref, info_ref, q_wide, k_all, v_all, k_sel, v_sel, pos, heads
    )
    weights = (weights / total).astype(jnp.bfloat16)
    blended = dot(weights, v_sel[...], TN)
    for h in range(heads):
        cols = slice(h * HD, (h + 1) * HD)
        o_ref[:, cols] = blended[h * BS : (h + 1) * BS, cols].astype(jnp.bfloat16)


def backward_kernel(
    heads, cycle, sel_ref, place_ref, info_ref, q_ref, g_ref, k_all, v_all, dq_ref, *rest
):
    own_ref, far_refs = rest[0], rest[1:cycle]
    dk_sum, dv_sum, q_wide, g_wide, k_sel, v_sel, pos = rest[cycle:]
    block = pl.program_id(0)

    @pl.when(block == 0)
    def _():
        q_wide[...] = jnp.zeros_like(q_wide)
        g_wide[...] = jnp.zeros_like(g_wide)
        dk_sum[...] = jnp.zeros_like(dk_sum)
        dv_sum[...] = jnp.zeros_like(dv_sum)

    spread(q_ref, q_wide, heads)
    spread(g_ref, g_wide, heads)
    weights, total = student_weights(
        sel_ref, place_ref, info_ref, q_wide, k_all, v_all, k_sel, v_sel, pos, heads
    )
    weights = weights / total
    weight_grad = dot(v_sel[...], g_wide[...], NT)
    row_dots = jnp.sum(weights * weight_grad, axis=0, keepdims=True)
    score_grad = (weights * (weight_grad - row_dots) * SCALE).astype(jnp.bfloat16)
    query_grad = dot(score_grad, k_sel[...], TN)
    for h in range(heads):
        cols = slice(h * HD, (h + 1) * HD)
        dq_ref[:, cols] = query_grad[h * BS : (h + 1) * BS, cols]
    key_grad = dot(score_grad, q_wide[...])
    value_grad = dot(weights.astype(jnp.bfloat16), g_wide[...])
    for e in range(sel_ref.shape[1]):
        target = pl.ds(pl.multiple_of(place_ref[block, e] * BS, BS), BS)
        dk_sum[target, :] += key_grad[e * BS : (e + 1) * BS, :]
        dv_sum[target, :] += value_grad[e * BS : (e + 1) * BS, :]

    @pl.when(block == pl.num_programs(0) - 1)
    def _():
        rows = own_ref.shape[1]
        own_ref[0] = dk_sum[:rows, :]
        own_ref[1] = dv_sum[:rows, :]
        for d in range(1, cycle):
            far_refs[d - 1][0] = dk_sum[d * rows : (d + 1) * rows, :].astype(jnp.bfloat16)
            far_refs[d - 1][1] = dv_sum[d * rows : (d + 1) * rows, :].astype(jnp.bfloat16)


def student_scratch(heads, keys, wides):
    width = heads * HD
    return [pltpu.VMEM((heads * BS, width), jnp.bfloat16)] * wides + [
        pltpu.VMEM((keys, width), jnp.bfloat16),
        pltpu.VMEM((keys, width), jnp.bfloat16),
        pltpu.VMEM((keys, heads * BS), jnp.int32),
    ]


def student_forward(tables, queries, keys, values):
    rows, width = queries.shape
    tokens = keys.shape[0]
    heads = width // HD
    row_block = pl.BlockSpec((BS, width), lambda b, *_: (b, 0))
    whole = pl.BlockSpec((tokens, width), lambda b, *_: (0, 0))
    return pl.pallas_call(
        functools.partial(forward_kernel, heads),
        grid_spec=pltpu.PrefetchScalarGridSpec(
            num_scalar_prefetch=3,
            grid=(rows // BS,),
            in_specs=[row_block, whole, whole],
            out_specs=row_block,
            scratch_shapes=student_scratch(heads, tables[0].shape[1] * BS, 1),
        ),
        out_shape=jax.ShapeDtypeStruct((rows, width), jnp.bfloat16),
        compiler_params=pltpu.CompilerParams(vmem_limit_bytes=VMEM_LIMIT),
        cost_estimate=pl.CostEstimate(
            flops=16 * rows * tokens * width, bytes_accessed=4 * tokens * width, transcendentals=0
        ),
    )(*tables, queries, keys, values)


def student_backward(tables, queries, grads, keys, values):
    rows, width = queries.shape
    tokens = keys.shape[0]
    cycle = tokens // rows
    heads = width // HD
    row_block = pl.BlockSpec((BS, width), lambda b, *_: (b, 0))
    whole = pl.BlockSpec((tokens, width), lambda b, *_: (0, 0))
    pair = pl.BlockSpec((2, rows, width), lambda b, *_: (0, 0, 0))
    return pl.pallas_call(
        functools.partial(backward_kernel, heads, cycle),
        grid_spec=pltpu.PrefetchScalarGridSpec(
            num_scalar_prefetch=3,
            grid=(rows // BS,),
            in_specs=[row_block, row_block, whole, whole],
            out_specs=[row_block] + [pair] * cycle,
            scratch_shapes=[pltpu.VMEM((tokens, width), jnp.float32)] * 2
            + student_scratch(heads, tables[0].shape[1] * BS, 2),
        ),
        out_shape=[
            jax.ShapeDtypeStruct((rows, width), jnp.float32),
            jax.ShapeDtypeStruct((2, rows, width), jnp.float32),
        ]
        + [jax.ShapeDtypeStruct((2, rows, width), jnp.bfloat16)] * (cycle - 1),
        compiler_params=pltpu.CompilerParams(vmem_limit_bytes=VMEM_LIMIT),
        cost_estimate=pl.CostEstimate(
            flops=32 * rows * tokens * width, bytes_accessed=8 * tokens * width, transcendentals=0
        ),
    )(*tables, queries, grads, keys, values)


def project_kernel(s_attn, t_attn, s_out, t_out, o_ref):
    o_ref[0] = (dot(s_attn[...], s_out[...]) - dot(t_attn[...], t_out[...])).astype(jnp.bfloat16)


def project(s_attn, t_attn, s_out, t_out, groups):
    rows = s_attn.shape[0]
    model = s_out.shape[1]
    tile = model // groups
    return pl.pallas_call(
        project_kernel,
        grid=(groups,),
        in_specs=[
            pl.BlockSpec(s_attn.shape, lambda j: (0, 0)),
            pl.BlockSpec(t_attn.shape, lambda j: (0, 0)),
            pl.BlockSpec((s_attn.shape[1], tile), lambda j: (0, j)),
            pl.BlockSpec((t_attn.shape[1], tile), lambda j: (0, j)),
        ],
        out_specs=pl.BlockSpec((1, rows, tile), lambda j: (j, 0, 0)),
        out_shape=jax.ShapeDtypeStruct((groups, rows, tile), jnp.bfloat16),
        compiler_params=pltpu.CompilerParams(vmem_limit_bytes=VMEM_LIMIT),
    )(s_attn, t_attn, s_out, t_out)


def project_grads_kernel(t_width, s_attn, t_attn, mix, o_ref):
    pieces, rows, width = mix.shape
    columns = mix[...].reshape(pieces * rows, width)
    o_ref[0] = (
        dot(s_attn[...], columns[:, t_width:], NT) - dot(t_attn[...], columns[:, :t_width], NT)
    ).astype(jnp.bfloat16)


def project_grads(s_attn, t_attn, mix, groups):
    rows = s_attn.shape[0]
    pieces, depth, width = mix.shape
    tile = depth // groups
    return pl.pallas_call(
        functools.partial(project_grads_kernel, t_attn.shape[1]),
        grid=(groups,),
        in_specs=[
            pl.BlockSpec(s_attn.shape, lambda j: (0, 0)),
            pl.BlockSpec(t_attn.shape, lambda j: (0, 0)),
            pl.BlockSpec((pieces, tile, width), lambda j: (0, j, 0)),
        ],
        out_specs=pl.BlockSpec((1, rows, pieces * tile), lambda j: (j, 0, 0)),
        out_shape=jax.ShapeDtypeStruct((groups, rows, pieces * tile), jnp.bfloat16),
        compiler_params=pltpu.CompilerParams(vmem_limit_bytes=VMEM_LIMIT),
    )(s_attn, t_attn, mix)


def from_earlier(rows, distance):
    route = [(i - distance, i) for i in range(distance, lax.axis_size("blk"))]
    return lax.ppermute(rows, "blk", route)


MESH = pl.DeviceIdType.MESH


def greet(blk, grp, cycle, cores, pos=None, line=1):
    barrier = pltpu.get_barrier_semaphore()
    for d in range(cycle):
        for e in range(cores):
            if d or e:
                pl.semaphore_signal(
                    barrier,
                    inc=1,
                    device_id={"blk": lax.rem(blk + d, cycle), "grp": lax.rem(grp + e, cores)},
                    device_id_type=MESH,
                )
    ends = 0
    if pos is not None:
        for ahead, there in ((-1, pos > 0), (1, pos < line - 1)):
            @pl.when(there)
            def _():
                pl.semaphore_signal(
                    barrier, inc=1, device_id={"head": pos + ahead}, device_id_type=MESH
                )

            ends = ends + jnp.where(there, 1, 0)
    pl.semaphore_wait(barrier, cycle * cores - 1 + ends)


def send(src, dst, send_sem, recv_sem, blk, grp):
    return pltpu.make_async_remote_copy(
        src_ref=src,
        dst_ref=dst,
        send_sem=send_sem,
        recv_sem=recv_sem,
        device_id={"blk": blk, "grp": grp},
        device_id_type=MESH,
    )


def arrive_kernel(
    cycle, cores, line, picks, tq, tk, tv, sq, sk, sv, ints, t_hbm, s_hbm,
    oq, ok, ov, pq, pk, pv, oints, info, mix, blended,
    t_stage, s_stage, rows_all, t_w, s_w, table, q_wide, k_sel, v_sel,
    local, w_sem, s_send, s_recv, x_send, x_recv, t_send, t_recv, i_send, i_recv,
    z_send, z_recv, zx_send, zx_recv,
):
    blk, grp, pos = lax.axis_index("blk"), lax.axis_index("grp"), lax.axis_index("head")
    rows = tq.shape[0]
    half = rows // cores
    share = cycle // cores
    owner = blk // share
    other = lax.rem(grp + 1, cores)
    depth = rows_all.shape[2]
    teacher_sets = ((tk, ok), (tv, ov), (tq, oq))
    own_columns = pl.ds(pl.multiple_of(blk * HD, HD), HD)
    own_rows = s_hbm.at[pl.ds(pl.multiple_of(blk * depth, depth), depth), :]

    loads = [
        pltpu.make_async_copy(src, dst, w_sem.at[n])
        for n, (src, dst) in enumerate(
            ((own_rows, rows_all.at[pos, grp]), (t_hbm, t_w), (s_hbm, s_w))
        )
    ]
    inward = [
        pltpu.make_async_copy(src.at[:, own_columns], t_stage.at[t], local.at[t])
        for t, (src, dst) in enumerate(teacher_sets)
    ]
    for load in loads + inward:
        load.start()
    greet(blk, grp, cycle, cores, pos, line)

    int_copies = [
        send(ints, oints.at[blk], i_send.at[d - 1], i_recv.at[d - 1], lax.rem(blk + d, cycle), grp)
        for d in range(1, cycle)
    ]
    for copy in int_copies:
        copy.start()
    oints[blk] = ints[...]

    per_half = half // BS

    def token_blocks(s, e):
        return pl.ds((s * cores + e) * per_half, per_half)

    def student_copy(t, j, e):
        columns = pl.ds(j * HD, HD)
        if t == 0:
            return sq.at[pl.ds(e * half, half), columns], pq.at[blk]
        src, dst = (sk, pk) if t == 1 else (sv, pv)
        return src.at[pl.ds(e * per_half, per_half), :, columns], dst.at[token_blocks(blk, e)]

    def student_send(t, j, e):
        return send(
            *student_copy(t, j, e), s_send.at[t, j, e], s_recv.at[t, blk], grp * share + j, e
        )

    pieces = [(t, j, e) for t in (1, 2, 0) for j in range(share) for e in range(cores)]

    def is_mine(j, e):
        return (grp * share + j == blk) & (grp == e)

    for t, j, e in pieces:
        @pl.when(jnp.logical_not(is_mine(j, e)))
        def _():
            student_send(t, j, e).start()

    def relay(way, step, origin, src):
        return pltpu.make_async_remote_copy(
            src_ref=src,
            dst_ref=rows_all.at[origin, grp],
            send_sem=z_send.at[way, step],
            recv_sem=z_recv.at[origin],
            device_id={"head": pos + (1 if way == 0 else -1)},
            device_id_type=MESH,
        )

    def share_rows(origin, src):
        dst = rows_all.at[origin, grp]
        return send(src, dst, zx_send.at[origin], zx_recv.at[origin], blk, other)

    ahead = (pos < line - 1, pos > 0)

    for way in (0, 1):
        @pl.when(ahead[way])
        def _():
            relay(way, 0, pos, own_rows).start()

    share_rows(pos, own_rows).start()

    def relay_step(step):
        for way in (0, 1):
            origin = pos - step if way == 0 else pos + step
            exists = origin >= 0 if way == 0 else origin < line

            @pl.when(exists)
            def _():
                src = rows_all.at[origin, grp]
                pltpu.make_async_remote_copy(
                    src_ref=src,
                    dst_ref=src,
                    send_sem=z_send.at[way, step],
                    recv_sem=z_recv.at[origin],
                    device_id={"grp": other},
                    device_id_type=MESH,
                ).wait_recv()
                share_rows(origin, src).start()

                @pl.when(ahead[way])
                def _():
                    relay(way, step, origin, src).start()

    t_copies = []
    for t, (src, dst) in enumerate(teacher_sets):
        for d in range(1, cycle):
            dest = lax.rem(blk + d, cycle)
            columns = pl.ds(pl.multiple_of(dest * HD, HD), HD)
            t_copies.append(
                send(
                    src.at[:, columns], dst.at[blk], t_send.at[t, d - 1], t_recv.at[t, d - 1], dest, grp
                )
            )
    for copy in t_copies:
        copy.start()

    outward = [
        pltpu.make_async_copy(t_stage.at[t], dst.at[blk], local.at[t])
        for t, (src, dst) in enumerate(teacher_sets)
    ]
    for t in range(3):
        inward[t].wait()
        outward[t].start()
    for t in range(3):
        outward[t].wait()

    for t, j, e in pieces:
        @pl.when(is_mine(j, e))
        def _():
            src, dst = student_copy(t, j, e)
            copy = pltpu.make_async_copy(src, dst, local.at[t])
            copy.start()
            copy.wait()

    def piece_of(t, s):
        return (pq.at[s], pk.at[token_blocks(s, grp)], pv.at[token_blocks(s, grp)])[t]

    def cross(t, s):
        ref = piece_of(t, s)
        return send(ref, ref, x_send.at[t - 1, s], x_recv.at[t - 1, s], blk, other)

    for t in (1, 2, 0):
        for s in range(cycle):
            @pl.when(jnp.logical_not((s == blk) & (owner == grp)))
            def _():
                ref = piece_of(t, s)
                send(ref, ref, s_send.at[t, 0, 0], s_recv.at[t, s], other, other).wait_recv()

            if t:
                cross(t, s).start()
        if t == 1:
            relay_step(1)
    for copy in int_copies:
        copy.wait()
    to_table = pltpu.make_async_copy(oints, table, local.at[0])
    to_table.start()
    seg_rows = ints.shape[0] - rows // BS
    first_count = jnp.sum((oints[:, :seg_rows, :] == 0).astype(jnp.float32)).astype(jnp.int32)
    info[0] = 0
    info[1] = first_count
    info[2] = grp
    info[3] = 0
    q_wide[...] = jnp.zeros_like(q_wide)
    for t in (1, 2):
        for s in range(cycle):
            cross(t, s).wait()
    to_table.wait()

    mine = half // BS
    pairs = cycle * half // (2 * BS)

    def pair_step(pair, carry):
        @pl.when(pair == pairs // 8)
        def _():
            relay_step(2)

        source, inside = pair * 2 // mine, lax.rem(pair * 2, mine)
        first_row = pl.multiple_of(inside * BS, 2 * BS)
        spread_pair(pq.at[source, pl.ds(first_row, 2 * BS), :], q_wide)
        at = grp * mine + inside

        def chosen(h, e):
            return table[source, seg_rows + at + h, e]

        weights, total = pair_weights(
            chosen, picks, source * (rows // BS) + at, first_count, q_wide, pk, pv, k_sel, v_sel
        )
        weights = (weights / total).astype(jnp.bfloat16)
        value = dot(weights, v_sel[...], TN)
        for h in range(2):
            blended[source, pl.ds(first_row + h * BS, BS), :] = value[
                h * BS : (h + 1) * BS, h * HD : (h + 1) * HD
            ].astype(jnp.bfloat16)
        return carry

    lax.fori_loop(0, pairs, pair_step, 0)
    relay_step(3)

    for load in loads:
        load.wait()
    for origin in range(line):
        share_rows(origin, rows_all.at[origin, grp]).wait_recv()
    gathered = rows_all.shape[0] * rows_all.shape[1] * depth
    width = 2 * HD
    for w, base in ((t_w, 0), (s_w, t_w.shape[0])):
        def gram(n, carry):
            at = pl.multiple_of(n * width, width)
            value = dot(rows_all[...].reshape(gathered, w.shape[1]), w[pl.ds(at, width), :], NT)
            mix[:, pl.ds(pl.multiple_of(base + at, width), width)] = value.astype(jnp.bfloat16)
            return carry

        lax.fori_loop(0, w.shape[0] // width, gram, 0)

    for copy in t_copies:
        copy.wait()
    for t, j, e in pieces:
        @pl.when(jnp.logical_not(is_mine(j, e)))
        def _():
            student_send(t, j, e).wait_send()
    for origin in range(line):
        share_rows(origin, rows_all.at[origin, grp]).wait_send()
    for way in (0, 1):
        for step in range(line - 1):
            origin = pos - step if way == 0 else pos + step
            exists = origin >= 0 if way == 0 else origin < line

            @pl.when(exists & ahead[way])
            def _():
                relay(way, step, origin, rows_all.at[origin, grp]).wait_send()


def arrive(t_query, t_key, t_value, t_out, s_query, s_key, s_value, s_out, ints, picks, sizes):
    cycle, cores, line = sizes
    rows = t_query.shape[0]
    half = rows // cores
    share = cycle // cores
    depth = s_out.shape[0] // cycle
    kind = t_query.dtype
    any_space = pl.BlockSpec(memory_space=pl.ANY)
    vmem = pl.BlockSpec(memory_space=pltpu.VMEM)
    dma = pltpu.SemaphoreType.DMA
    return pl.pallas_call(
        functools.partial(arrive_kernel, cycle, cores, line, picks),
        in_specs=[any_space] * 6 + [vmem] + [any_space] * 2,
        out_specs=[any_space] * 3
        + [vmem] * 4
        + [pl.BlockSpec(memory_space=pltpu.SMEM)]
        + [vmem] * 2,
        out_shape=[jax.ShapeDtypeStruct((cycle, rows, HD), kind)] * 3
        + [jax.ShapeDtypeStruct((cycle, half, HD), kind)]
        + [jax.ShapeDtypeStruct((cycle * rows // BS, BS, HD), kind)] * 2
        + [
            jax.ShapeDtypeStruct((cycle,) + ints.shape, ints.dtype),
            jax.ShapeDtypeStruct((4,), jnp.int32),
            jax.ShapeDtypeStruct((line * cores * depth, t_out.shape[0] + s_out.shape[0]), kind),
            jax.ShapeDtypeStruct((cycle, half, HD), kind),
        ],
        scratch_shapes=[
            pltpu.VMEM((3, rows, HD), kind),
            pltpu.VMEM((half, HD), kind),
            pltpu.VMEM((line, cores, depth, s_out.shape[1]), kind),
            pltpu.VMEM(t_out.shape, kind),
            pltpu.VMEM(s_out.shape, kind),
            pltpu.SMEM((cycle,) + ints.shape, ints.dtype),
        ]
        + pair_scratch(picks * BS, 1)
        + [
            dma((3,)),
            dma((3,)),
            dma((3, share, cores)),
            dma((3, cycle)),
            dma((2, cycle)),
            dma((2, cycle)),
            dma((3, cycle - 1)),
            dma((3, cycle - 1)),
            dma((cycle - 1,)),
            dma((cycle - 1,)),
            dma((2, line)),
            dma((line,)),
            dma((line,)),
            dma((line,)),
        ],
        compiler_params=pltpu.CompilerParams(
            collective_id=0, has_side_effects=True, vmem_limit_bytes=VMEM_LIMIT
        ),
    )(t_query, t_key, t_value, s_query, s_key, s_value, ints, t_out, s_out)


def depart_kernel(
    cycle, cores, line, parts, dq, own, far, terms, out_q, out_k, out_v, m_out,
    got, mine, m_own, m_got, m_line, total,
    x_send, x_recv, d_send, d_recv, mx_send, mx_recv, mz_send, mz_recv,
):
    blk, grp, pos = lax.axis_index("blk"), lax.axis_index("grp"), lax.axis_index("head")
    half = dq.shape[1]
    share = cycle // cores
    owner, slot = blk // share, lax.rem(blk, share)
    other = lax.rem(grp + 1, cores)
    step = m_own.shape[2]
    greet(blk, grp, cycle, cores, pos, line)

    def target(t, j, e):
        rows = pl.ds(pl.multiple_of(e * half, half), half)
        return (out_q, out_k, out_v)[t].at[rows, pl.ds(pl.multiple_of(j * HD, HD), HD)]

    def source(t, s):
        return dq.at[s] if t == 0 else mine.at[t - 1, s]

    def piece(t, s):
        return send(
            source(t, s), target(t, slot, grp), d_send.at[t, s], d_recv.at[t, slot, grp], s, owner
        )

    def local(s):
        return (s == blk) & (owner == grp)

    def emit(t, s):
        @pl.when(jnp.logical_not(local(s)))
        def _():
            piece(t, s).start()

        @pl.when(local(s))
        def _():
            target(t, slot, grp)[...] = source(t, s)[...]

    def term_cross(n, z):
        return send(
            terms.at[z * cores + other, pl.ds(n * step, step), :],
            m_got.at[n, z],
            mx_send.at[n, z],
            mx_recv.at[n, z],
            blk,
            other,
        )

    def hop(n, way, dest, there):
        return pltpu.make_async_remote_copy(
            src_ref=m_own.at[n, dest],
            dst_ref=m_line.at[way, n, dest],
            send_sem=mz_send.at[n, dest],
            recv_sem=mz_recv.at[way, n, dest],
            device_id={"head": there},
            device_id_type=MESH,
        )

    def fold(n):
        for z in range(line):
            term_cross(n, z).wait_recv()
            m_own[n, z] = (
                terms[z * cores + grp, pl.ds(n * step, step), :].astype(jnp.float32)
                + m_got[n, z].astype(jnp.float32)
            ).astype(jnp.bfloat16)

    def flow(n, upward):
        way = jnp.where(upward, 0, 1)
        there = jnp.where(upward, pos + 1, pos - 1)
        count = jnp.where(upward, line - 1 - pos, pos)
        fed = jnp.where(upward, pos, line - 1 - pos) > 0

        def body(k, carry):
            dest = jnp.where(upward, line - 1 - k, k)

            @pl.when(fed)
            def _():
                hop(n, way, dest, there).wait_recv()
                m_own[n, dest] = (
                    m_own[n, dest].astype(jnp.float32) + m_line[way, n, dest].astype(jnp.float32)
                ).astype(jnp.bfloat16)

            hop(n, way, dest, there).start()
            return carry

        lax.fori_loop(0, count, body, 0)

    def final(n):
        total[...] = m_own[n, pos].astype(jnp.float32)
        for way, fed in ((0, pos > 0), (1, pos < line - 1)):
            @pl.when(fed)
            def _():
                hop(n, way, pos, pos).wait_recv()
                total[...] += m_line[way, n, pos].astype(jnp.float32)

        m_out[n * step : (n + 1) * step, :] = total[...]

    crossing = [
        send(far.at[t], got.at[t], x_send.at[t], x_recv.at[t], blk, other) for t in range(2)
    ]
    for z in range(line):
        term_cross(0, z).start()
    for copy in crossing:
        copy.start()
    for n in range(1, parts):
        for z in range(line):
            term_cross(n, z).start()
    for s in range(cycle):
        emit(0, s)
    low = pos < line // 2
    fold(0)
    flow(0, low)
    for t in range(2):
        crossing[t].wait_recv()
        for s in range(cycle):
            mine[t, s] = (own[t, s] + got[t, s].astype(jnp.float32)).astype(jnp.bfloat16)
        for s in range(cycle):
            emit(t + 1, s)
    for n in range(parts + 1):
        if 0 < n < parts:
            fold(n)
            flow(n, low)
        if n:
            flow(n - 1, jnp.logical_not(low))
    for n in range(parts):
        final(n)
    for copy in crossing:
        copy.wait_send()
    for t in range(3):
        for j in range(share):
            for e in range(cores):
                ours = (grp * share + j == blk) & (grp == e)

                @pl.when(jnp.logical_not(ours))
                def _():
                    ref = target(t, j, e)
                    send(ref, ref, d_send.at[t, 0], d_recv.at[t, j, e], blk, other).wait_recv()

    for t in range(3):
        for s in range(cycle):
            @pl.when(jnp.logical_not(local(s)))
            def _():
                piece(t, s).wait_send()

    for n in range(parts):
        for dest in range(line):
            term_cross(n, dest).wait_send()

            @pl.when(dest != pos)
            def _():
                hop(n, 0, dest, other).wait_send()


def depart(dq, own, far, terms, cycle, cores, line):
    half = dq.shape[1]
    share = cycle // cores
    parts = 2
    rows, wide = terms.shape[1:]
    step = rows // parts
    kind = jnp.bfloat16
    vmem = pl.BlockSpec(memory_space=pltpu.VMEM)
    dma = pltpu.SemaphoreType.DMA
    block = (parts, line, step, wide)
    return pl.pallas_call(
        functools.partial(depart_kernel, cycle, cores, line, parts),
        in_specs=[vmem] * 4,
        out_specs=[vmem] * 4,
        out_shape=[jax.ShapeDtypeStruct((cores * half, share * HD), kind)] * 3
        + [jax.ShapeDtypeStruct((rows, wide), jnp.float32)],
        scratch_shapes=[
            pltpu.VMEM((2, cycle, half, HD), kind),
            pltpu.VMEM((2, cycle, half, HD), kind),
            pltpu.VMEM(block, kind),
            pltpu.VMEM(block, kind),
            pltpu.VMEM((2,) + block, kind),
            pltpu.VMEM((step, wide), jnp.float32),
            dma((2,)),
            dma((2,)),
            dma((3, cycle)),
            dma((3, share, cores)),
            dma((parts, line)),
            dma((parts, line)),
            dma((parts, line)),
            dma((2, parts, line)),
        ],
        compiler_params=pltpu.CompilerParams(
            collective_id=1, has_side_effects=True, vmem_limit_bytes=VMEM_LIMIT
        ),
    )(dq, own, far, terms)


def pair_weights(
    chosen, count, query_block, first_count, q_wide, k_all, v_all, k_sel, v_sel
):
    for e in range(count):
        for h in range(2):
            source = chosen(h, e)
            cols = slice(h * HD, (h + 1) * HD)
            k_sel[e * BS : (e + 1) * BS, cols] = k_all[source]
            v_sel[e * BS : (e + 1) * BS, cols] = v_all[source]
    within = lax.broadcasted_iota(jnp.int32, (BS, 1), 0)
    lane = lax.broadcasted_iota(jnp.int32, (1, 2 * BS), 1)
    second = lane >= BS
    query_pos = query_block * BS + lane
    low = jnp.where(query_pos < first_count, 0, first_count)
    scores = dot(k_sel[...], q_wide[...], NT)
    allowed = []
    for e in range(count):
        base = jnp.where(second, chosen(1, e), chosen(0, e)) * BS
        allowed.append((within <= query_pos - base) & (within >= low - base))
    scores = jnp.concatenate(
        [jnp.where(a, scores[e * BS : (e + 1) * BS], MASKED) for e, a in enumerate(allowed)]
    )
    largest = jnp.max(scores, axis=0, keepdims=True)
    weights = jnp.exp2((scores - largest) * (SCALE * LOG2E))
    weights = jnp.concatenate(
        [jnp.where(a, weights[e * BS : (e + 1) * BS], 0.0) for e, a in enumerate(allowed)]
    )
    return weights, jnp.sum(weights, axis=0, keepdims=True)


def spread_pair(ref, scratch):
    for h in range(2):
        scratch[h * BS : (h + 1) * BS, h * HD : (h + 1) * HD] = ref[h * BS : (h + 1) * BS, :].astype(
            scratch.dtype
        )


def pair_backward_kernel(
    picks, rows, table, info_ref, q_ref, g_ref, k_all, v_all, dq_ref, own_ref, far_ref,
    dk_sum, dv_sum, q_wide, g_wide, k_sel, v_sel,
):
    pair = pl.program_id(0)

    @pl.when(pair == 0)
    def _():
        q_wide[...] = jnp.zeros_like(q_wide)
        g_wide[...] = jnp.zeros_like(g_wide)
        dk_sum[...] = jnp.zeros_like(dk_sum)
        dv_sum[...] = jnp.zeros_like(dv_sum)

    spread_pair(q_ref, q_wide)
    spread_pair(g_ref, g_wide)
    cycle, half = own_ref.shape[1], own_ref.shape[2]
    mine = half // BS
    source, inside = pair * 2 // mine, lax.rem(pair * 2, mine)
    at = info_ref[2] * mine + inside
    seg_rows = table.shape[1] - rows // BS

    def chosen(h, e):
        return table[source, seg_rows + at + h, e]

    weights, total = pair_weights(
        chosen, picks, source * (rows // BS) + at, info_ref[1], q_wide, k_all, v_all, k_sel, v_sel
    )
    weights = weights / total
    weight_grad = dot(v_sel[...], g_wide[...], NT)
    row_dots = jnp.sum(weights * weight_grad, axis=0, keepdims=True)
    score_grad = (weights * (weight_grad - row_dots) * SCALE).astype(jnp.bfloat16)
    query_grad = dot(score_grad, k_sel[...], TN)
    for h in range(2):
        dq_ref[h * BS : (h + 1) * BS, :] = query_grad[
            h * BS : (h + 1) * BS, h * HD : (h + 1) * HD
        ].astype(jnp.bfloat16)
    key_grad = dot(score_grad, q_wide[...])
    value_grad = dot(weights.astype(jnp.bfloat16), g_wide[...])
    for e in range(picks):
        for h in range(2):
            target = pl.ds(pl.multiple_of(chosen(h, e) * BS, BS), BS)
            cols = slice(h * HD, (h + 1) * HD)
            dk_sum[target, :] += key_grad[e * BS : (e + 1) * BS, cols]
            dv_sum[target, :] += value_grad[e * BS : (e + 1) * BS, cols]

    @pl.when(pair == pl.num_programs(0) - 1)
    def _():
        for s in range(cycle):
            near = pl.ds(pl.multiple_of(s * rows + info_ref[2] * half, half), half)
            away = pl.ds(pl.multiple_of((s + 1) * rows - (info_ref[2] + 1) * half, half), half)
            for t, total in enumerate((dk_sum, dv_sum)):
                own_ref[t, s] = total[near, :]
                far_ref[t, s] = total[away, :].astype(jnp.bfloat16)


def pair_scratch(keys, wides):
    return [pltpu.VMEM((2 * BS, 2 * HD), jnp.bfloat16)] * wides + [
        pltpu.VMEM((keys, 2 * HD), jnp.bfloat16),
        pltpu.VMEM((keys, 2 * HD), jnp.bfloat16),
    ]


def pair_backward(table, info, picks, queries, grads, keys, values):
    cycle, half, width = queries.shape
    tokens = keys.shape[0] * BS
    per_step = half // (2 * BS)
    row_block = pl.BlockSpec((None, 2 * BS, width), lambda b, *_: (b // per_step, b % per_step, 0))
    whole = pl.BlockSpec(keys.shape, lambda b, *_: (0, 0, 0))
    both = pl.BlockSpec((2, cycle, half, width), lambda b, *_: (0, 0, 0, 0))
    return pl.pallas_call(
        functools.partial(pair_backward_kernel, picks, tokens // cycle),
        grid_spec=pltpu.PrefetchScalarGridSpec(
            num_scalar_prefetch=2,
            grid=(cycle * per_step,),
            in_specs=[row_block, row_block, whole, whole],
            out_specs=[row_block, both, both],
            scratch_shapes=[pltpu.VMEM((tokens, width), jnp.float32)] * 2
            + pair_scratch(picks * BS, 2),
        ),
        out_shape=[
            jax.ShapeDtypeStruct((cycle, half, width), jnp.bfloat16),
            jax.ShapeDtypeStruct((2, cycle, half, width), jnp.float32),
            jax.ShapeDtypeStruct((2, cycle, half, width), jnp.bfloat16),
        ],
        compiler_params=pltpu.CompilerParams(vmem_limit_bytes=VMEM_LIMIT),
        cost_estimate=pl.CostEstimate(
            flops=32 * cycle * half * tokens * width,
            bytes_accessed=8 * tokens * width,
            transcendentals=0,
        ),
    )(table, info, queries, grads, keys, values)


def combine_kernel(
    cycle, cores, line, chunks, kept, heads_t, heads_s, mix_hbm, t_hbm, s_hbm,
    g_out, m_out, terms,
    mix, t_w, s_w, t_attn, s_attn, g_own, g_far, g_got, g_line, m_own, m_far, m_got, m_line,
    total, g_done, w_sem, t_send, t_recv, t_local, s_send, s_recv, s_local,
    gx_send, gx_recv, gz_send, gz_recv, mx_send, mx_recv, mz_send, mz_recv, d_send, d_recv,
    p_send, p_recv,
):
    blk, grp, pos = lax.axis_index("blk"), lax.axis_index("grp"), lax.axis_index("head")
    share = cycle // cores
    owner, slot = blk // share, lax.rem(blk, share)
    other = lax.rem(grp + 1, cores)
    step = t_attn.shape[0] // chunks
    per_half = chunks // cores

    loads = [
        pltpu.make_async_copy(src, dst, w_sem.at[n])
        for n, (src, dst) in enumerate(((mix_hbm, mix.at[blk]), (t_hbm, t_w), (s_hbm, s_w)))
    ]
    for load in loads:
        load.start()

    greet(blk, grp, cycle, cores, pos, line)

    def t_copy(i, d):
        dest = lax.rem(blk + d, cycle)
        src = heads_t.at[dest, pl.ds(i * step, step), :]
        dst = t_attn.at[pl.ds(i * step, step), pl.ds(pl.multiple_of(blk * HD, HD), HD)]
        if d == 0:
            return pltpu.make_async_copy(src, dst, t_local.at[i])
        return send(src, dst, t_send.at[i, d - 1], t_recv.at[i, d - 1], dest, grp)

    def s_ends(r, s):
        rows = pl.ds(pl.multiple_of((grp * per_half + r) * step, step), step)
        dst = s_attn.at[rows, pl.ds(pl.multiple_of(slot * HD, HD), HD)]
        return heads_s.at[s, pl.ds(r * step, step), :], dst

    def s_copy(r, s):
        return send(
            *s_ends(r, s), s_send.at[r, s], s_recv.at[slot, grp * per_half + r], s, owner
        )

    def s_here(r, s):
        return pltpu.make_async_copy(*s_ends(r, s), s_local.at[r])

    mix_copies = [
        send(mix_hbm, mix.at[blk], p_send.at[d - 1], p_recv.at[d - 1], lax.rem(blk + d, cycle), grp)
        for d in range(1, cycle)
    ]
    for i in range(chunks):
        if i == min(kept, chunks - 1):
            for copy in mix_copies:
                copy.start()
        for d in range(cycle):
            t_copy(i, d).start()
        if i < per_half:
            for s in range(cycle):
                here = (s == blk) & (owner == grp)

                @pl.when(here)
                def _():
                    s_here(i, s).start()

                @pl.when(jnp.logical_not(here))
                def _():
                    s_copy(i, s).start()

    def await_inputs(i):
        for d in range(1, cycle):
            t_copy(i, d).wait_recv()
        t_copy(i, 0).wait()
        e, r = i // per_half, i % per_half
        for j in range(share):
            here = (grp * share + j == blk) & (grp == e)

            @pl.when(here)
            def _():
                s_here(r, grp * share + j).wait()

            @pl.when(jnp.logical_not(here))
            def _():
                ref = s_attn.at[pl.ds(i * step, step), pl.ds(j * HD, HD)]
                send(ref, ref, s_send.at[r, 0], s_recv.at[j, i], blk, other).wait_recv()

    t_width, s_width = t_attn.shape[1], s_attn.shape[1]

    def rows_of(i):
        rows = pl.ds(i * step, step)
        return t_attn[rows, :], s_attn[rows, :]

    def grad_term(i, group):
        t_rows, s_rows = rows_of(i)
        depth = mix.shape[1] // (line * cores)
        part = mix[:, pl.ds(pl.multiple_of(group * depth, depth), depth), :]
        part = part.reshape(mix.shape[0] * depth, mix.shape[2])
        value = dot(s_rows, part[:, t_width:], NT) - dot(t_rows, part[:, :t_width], NT)
        return value.astype(jnp.bfloat16)

    def out_term(i, group):
        t_rows, s_rows = rows_of(i)
        width = t_w.shape[1] // (line * cores)
        cols = pl.ds(pl.multiple_of(group * width, width), width)
        return (dot(s_rows, s_w[:, cols]) - dot(t_rows, t_w[:, cols])).astype(jnp.bfloat16)

    kinds = {
        "g": (grad_term, g_own, g_far, g_got, g_line, gx_send, gx_recv, gz_send, gz_recv),
        "m": (out_term, m_own, m_far, m_got, m_line, mx_send, mx_recv, mz_send, mz_recv),
    }

    def cross(kind, i):
        _, _, far, got, _, x_send, x_recv, _, _ = kinds[kind]
        return send(far.at[i], got.at[i], x_send.at[i], x_recv.at[i], blk, other)

    def hop(kind, i, way, dest, target):
        _, own, _, _, relay, _, _, z_send, z_recv = kinds[kind]
        return pltpu.make_async_remote_copy(
            src_ref=own.at[i, dest],
            dst_ref=relay.at[way, i, dest],
            send_sem=z_send.at[i, dest],
            recv_sem=z_recv.at[way, i, dest],
            device_id={"head": target},
            device_id_type=MESH,
        )

    def compute(kind, i):
        if kind == "m" or i >= kept:
            await_inputs(i)
        if (kind, i) == ("g", 0):
            loads[0].wait()
            for copy in mix_copies:
                copy.wait()
        if (kind, i) == ("m", 0):
            loads[1].wait()
            loads[2].wait()
        term, own, far = kinds[kind][:3]

        def body(z, carry):
            far[i, z] = term(i, z * cores + other)
            own[i, z] = term(i, z * cores + grp)
            return carry

        lax.fori_loop(0, line, body, 0)
        cross(kind, i).start()

    def add(kind, i, dest, ref):
        own = kinds[kind][1]
        own[i, dest] = (
            own[i, dest].astype(jnp.float32) + ref[...].astype(jnp.float32)
        ).astype(jnp.bfloat16)

    def fold(kind, i):
        got = kinds[kind][3]
        cross(kind, i).wait_recv()

        def body(z, carry):
            add(kind, i, z, got.at[i, z])
            return carry

        lax.fori_loop(0, line, body, 0)

    def flow(kind, i, upward):
        way = jnp.where(upward, 0, 1)
        target = jnp.where(upward, pos + 1, pos - 1)
        count = jnp.where(upward, line - 1 - pos, pos)
        fed = jnp.where(upward, pos, line - 1 - pos) > 0
        relay = kinds[kind][4]

        def body(k, carry):
            dest = jnp.where(upward, line - 1 - k, k)

            @pl.when(fed)
            def _():
                hop(kind, i, way, dest, target).wait_recv()
                add(kind, i, dest, relay.at[way, i, dest])

            hop(kind, i, way, dest, target).start()
            return carry

        lax.fori_loop(0, count, body, 0)

    def final(kind, i):
        own, relay = kinds[kind][1], kinds[kind][4]
        width = own.shape[3]
        total[:, :width] = own[i, pos].astype(jnp.float32)
        for way, fed in ((0, pos > 0), (1, pos < line - 1)):
            @pl.when(fed)
            def _():
                hop(kind, i, way, pos, pos).wait_recv()
                total[:, :width] += relay[way, i, pos].astype(jnp.float32)

        if kind == "m":
            m_out[pl.ds(i * step, step), :] = total[...]
            return
        for j in range(share):
            g_done[i, j] = total[:, j * HD : (j + 1) * HD].astype(jnp.bfloat16)
            here = (grp * share + j == blk) & (grp == i // per_half)

            @pl.when(here)
            def _():
                g_out[blk, pl.ds(i % per_half * step, step), :] = g_done[i, j]

            @pl.when(jnp.logical_not(here))
            def _():
                deliver(i, j).start()

    def deliver(i, j):
        r = i % per_half
        return send(
            g_done.at[i, j],
            g_out.at[blk, pl.ds(r * step, step), :],
            d_send.at[i, j],
            d_recv.at[blk, r],
            grp * share + j,
            i // per_half,
        )

    low = pos < line // 2
    items = [("m", i) for i in range(kept)] + [("g", i) for i in range(chunks)]
    for k in range(len(items) + 3):
        if k < len(items) and k != kept:
            compute(*items[k])
        if 0 <= k - 1 < len(items):
            fold(*items[k - 1])
            flow(*items[k - 1], low)
        if 0 <= k - 2 < len(items):
            flow(*items[k - 2], jnp.logical_not(low))
        if 0 <= k - 3 < len(items):
            final(*items[k - 3])
        if k == kept:
            compute(*items[k])
        if kept < chunks and k >= len(items) - 1:
            if not kept and k == len(items) - 1:
                loads[1].wait()
                loads[2].wait()
            part = line * cores // 4

            def body(n, carry):
                group = (k - len(items) + 1) * part + n
                for i in range(kept, chunks):
                    terms[group, pl.ds((i - kept) * step, step), :] = out_term(i, group)
                return carry

            lax.fori_loop(0, part, body, 0)

    for s in range(cycle):
        here = (s == blk) & (owner == grp)

        @pl.when(jnp.logical_not(here))
        def _():
            for r in range(per_half):
                ref = g_out.at[s, pl.ds(r * step, step), :]
                send(ref, ref, d_send.at[0, 0], d_recv.at[s, r], other, other).wait_recv()

    for i in range(chunks):
        for d in range(1, cycle):
            t_copy(i, d).wait_send()
        if i < per_half:
            for s in range(cycle):
                @pl.when(jnp.logical_not((s == blk) & (owner == grp)))
                def _():
                    s_copy(i, s).wait_send()
        for j in range(share):
            @pl.when(jnp.logical_not((grp * share + j == blk) & (grp == i // per_half)))
            def _():
                deliver(i, j).wait_send()

    for kind, i in items:
        cross(kind, i).wait_send()
        for dest in range(line):
            @pl.when(dest != pos)
            def _():
                hop(kind, i, 0, dest, other).wait_send()


def combine(heads_t, heads_s, mix, t_out, s_out, cycle, cores, line, kept):
    rows = heads_t.shape[1]
    chunks = 2 * cores
    step = rows // chunks
    share = cycle // cores
    groups = line * cores
    wide = t_out.shape[1] // groups
    t_width, s_width = t_out.shape[0], s_out.shape[0]
    half = rows // cores
    kind = jnp.bfloat16
    any_space = pl.BlockSpec(memory_space=pl.ANY)
    vmem = pl.BlockSpec(memory_space=pltpu.VMEM)
    dma = pltpu.SemaphoreType.DMA
    held = max(kept, 1)
    rest = max(chunks - kept, 1)

    def lines(n, width):
        block = (n, line, step, width)
        return [pltpu.VMEM(block, kind)] * 3 + [pltpu.VMEM((2,) + block, kind)]

    def line_sems(n):
        return [dma((n,)), dma((n,)), dma((n, line)), dma((2, n, line))]

    return pl.pallas_call(
        functools.partial(combine_kernel, cycle, cores, line, chunks, kept),
        in_specs=[any_space] * 5,
        out_specs=[vmem] * 3,
        out_shape=[
            jax.ShapeDtypeStruct((cycle, half, HD), kind),
            jax.ShapeDtypeStruct((held * step, wide), jnp.float32),
            jax.ShapeDtypeStruct((groups, rest * step, wide), kind),
        ],
        scratch_shapes=[
            pltpu.VMEM((cycle,) + mix.shape, kind),
            pltpu.VMEM(t_out.shape, kind),
            pltpu.VMEM(s_out.shape, kind),
            pltpu.VMEM((rows, t_width), kind),
            pltpu.VMEM((rows, s_width), kind),
        ]
        + lines(chunks, s_width)
        + lines(held, wide)
        + [
            pltpu.VMEM((step, wide), jnp.float32),
            pltpu.VMEM((chunks, share, step, HD), kind),
            dma((3,)),
            dma((chunks, cycle - 1)),
            dma((chunks, cycle - 1)),
            dma((chunks,)),
            dma((chunks // cores, cycle)),
            dma((share, chunks)),
            dma((chunks // cores,)),
        ]
        + line_sems(chunks)
        + line_sems(held)
        + [dma((chunks, share)), dma((cycle, chunks // cores)), dma((cycle - 1,)), dma((cycle - 1,))],
        compiler_params=pltpu.CompilerParams(
            collective_id=2, has_side_effects=True, vmem_limit_bytes=VMEM_LIMIT
        ),
        cost_estimate=pl.CostEstimate(
            flops=0, bytes_accessed=64 * rows * wide * groups, transcendentals=0
        ),
    )(heads_t, heads_s, mix, t_out, s_out)


def heads_on_chips(
    t_query, t_key, t_value, t_out, s_query, s_key, s_value, s_out, segments, selection
):
    rows = t_query.shape[0]
    cycle, cores, line = lax.axis_size("blk"), lax.axis_size("grp"), lax.axis_size("head")
    picks = selection.shape[1]

    lanes = 128
    ints = jnp.concatenate(
        [segments.reshape(rows // lanes, lanes), jnp.pad(selection, ((0, 0), (0, lanes - picks)))]
    )
    tq, tk, tv, pq, pk, pv, table, info, mix, blended = arrive(
        t_query, t_key, t_value, t_out, s_query,
        s_key.reshape(rows // BS, BS, -1), s_value.reshape(rows // BS, BS, -1),
        s_out, ints, picks, (cycle, cores, line),
    )
    whole = [x.reshape(cycle * rows, HD) for x in (tq, tk, tv)]
    whole_heads = teacher(info, *whole, 1, (1, (0, 0, 0)))

    kept = 3
    grads, near, terms = combine(
        whole_heads.reshape(cycle, rows, HD), blended, mix, t_out, s_out, cycle, cores, line, kept
    )
    dq, own, far = pair_backward(table, info, picks, pq, grads, pk, pv)
    *out, rest = depart(dq, own, far, terms, cycle, cores, line)
    mismatch = jnp.concatenate([near, rest])
    return (mismatch, *(x.astype(jnp.float32) for x in out))


def on_device(t_query, t_key, t_value, t_out, s_query, s_key, s_value, s_out, segments, selection):
    row_count = t_query.shape[0]
    heads = t_query.shape[1] // HD
    cycle = lax.axis_size("blk")
    split = ("head", "grp")
    groups = lax.axis_size("head") * lax.axis_size("grp")
    cores = lax.axis_size("grp")
    if cores == 2 and heads == cycle and s_query.shape[1] // HD * cores == cycle:
        return heads_on_chips(
            t_query, t_key, t_value, t_out, s_query, s_key, s_value, s_out, segments, selection
        )
    my_index = lax.axis_index("blk")
    first_row = my_index * row_count
    shard_blocks = row_count // BS

    count = jnp.sum((segments == 0).astype(jnp.int32)).reshape(1)
    first_count = count
    for distance in range(1, cycle):
        route = [(i, (i + distance) % cycle) for i in range(cycle)]
        first_count = first_count + lax.ppermute(count, "blk", route)
    first_count = first_count[0]
    info = jnp.stack([first_row, first_count]).astype(jnp.int32)

    piece = s_out.shape[0] // cycle
    s_rows = lax.dynamic_slice_in_dim(s_out, my_index * piece, piece, 0)
    s_rows = lax.all_gather(s_rows, split, axis=0, tiled=True)
    mix = jnp.concatenate([dot(s_rows, t_out, NT), dot(s_rows, s_out, NT)], axis=1)
    mix = lax.all_gather(mix.astype(jnp.bfloat16), "blk")

    if heads % cycle == 0:
        packed = jnp.concatenate(
            [rows.reshape(row_count, heads, HD) for rows in (t_query, t_key, t_value)], axis=2
        ).reshape(row_count, 3 * heads * HD)
        packed = lax.all_to_all(packed, "blk", split_axis=1, concat_axis=0, tiled=True)
        packed, s_key, s_value = lax.optimization_barrier((packed, s_key, s_value))
        start = jnp.stack([jnp.int32(0), first_count]).astype(jnp.int32)
        whole_heads = teacher(
            start, packed, packed, packed, heads // cycle, (3, (0, 1, 2))
        )
        t_attn = lax.all_to_all(whole_heads, "blk", split_axis=0, concat_axis=1, tiled=True)
    else:
        t_attn = teacher(
            info,
            t_query,
            lax.all_gather(t_key, "blk", axis=0, tiled=True),
            lax.all_gather(t_value, "blk", axis=0, tiled=True),
            heads,
            (1, (0, 0, 0)),
        )

    key_stack = jnp.concatenate([s_key] + [from_earlier(s_key, d) for d in range(1, cycle)])
    value_stack = jnp.concatenate([s_value] + [from_earlier(s_value, d) for d in range(1, cycle)])
    place = (my_index - selection // shard_blocks) * shard_blocks + selection % shard_blocks
    tables = (selection, place, info)
    s_attn = student_forward(tables, s_query, key_stack, value_stack)

    grad_terms = project_grads(s_attn, t_attn, mix, groups)
    grads = lax.psum_scatter(grad_terms, split, scatter_dimension=0, tiled=False)
    terms = project(s_attn, t_attn, s_out, t_out, groups)
    terms, grads = lax.optimization_barrier((terms, grads))
    mismatch = lax.psum_scatter(terms, split, scatter_dimension=0, tiled=False)

    grad_query, own, *far = student_backward(
        tables, s_query, grads, key_stack, value_stack
    )
    for distance in range(1, cycle):
        route = [(i, i - distance) for i in range(distance, cycle)]
        own = own + lax.ppermute(far[distance - 1], "blk", route).astype(jnp.float32)
    return (mismatch.astype(jnp.float32), grad_query, own[0], own[1])


def solution(mesh):
    split = ("head", "grp")
    tokens, weights = P("blk", split), P(split, None)
    return jax.shard_map(
        on_device,
        mesh=mesh,
        in_specs=(
            tokens, tokens, tokens, weights, tokens, tokens, tokens, weights, P("blk"),
            P("blk", None),
        ),
        out_specs=(tokens,) * 4,
        check_vma=False,
    )
```
